512 devices in a mesh: dp: 8 (over z_lo, core), gx: 64 (over y, x, z_hi).
Axes of the slice: x: 4, y: 8, z: 8 (z_hi: 2, z_lo: 4; z = z_hi * 4 + z_lo), core: 2. Of those that a mesh axis runs over, the one named last changes fastest.
Arguments:
- field: bfloat16 [8, 64, 32, 128, 128], P('dp', 'gx'), may hold values from -6 to 6
- cotangent: bfloat16 [8, 64, 32, 128, 128], P('dp', 'gx'), may hold values from -6 to 6
- spectral_weight: bfloat16 [512, 32, 2048], P('gx'), may hold values from -3 to 3
- pointwise_weight: bfloat16 [32, 32], replicated, may hold values from -1 to 1
Outputs:
- field_grad: bfloat16 [8, 64, 32, 128, 128], P('dp', 'gx')
- weight_grad: float32 [512, 32, 2048], P('gx', 'dp')
The draws below stay inside these ranges and needn't reach their ends.
All inputs are finite; a program needn't handle non-finite values.
Results may differ from the reference program's by a relative error of at most 0.001.
Values sent between devices are 32-bit elements; how exact they have to be, the bound alone decides.
A program may use at most 64 MiB of HBM per device.

```python
import jax
import jax.numpy as jnp
from jax import lax

C = 32
M = 16
NY = 128
NZ = 128
NX = 64
MX = 16
KX = 32
PAIRS = 512
SAMPLES = 8


def level_of(stream_key, extent, cuts, low, high):
    level, own = 1.0, jax.random.fold_in(stream_key, 6)
    for dim, parts in cuts:
        draws = jnp.exp(jax.random.uniform(jax.random.fold_in(own, dim), (parts,), jnp.float32, low / len(cuts), high / len(cuts)))
        level = level * jnp.repeat(draws, extent[dim] // parts).reshape([-1 if axis == dim else 1 for axis in range(len(extent))])
    return level


def bell_draw(key, dims, spread, bound, pieces=(), kind=jnp.bfloat16):
    result = jax.random.normal(key, dims, jnp.float32) * spread
    if len(pieces) > 0:
        result = level_of(key, dims, pieces, -0.22, 0.18) * result
    return jnp.clip(result, min=-bound, max=bound).astype(kind)


def setup_inputs(seed: int = 0) -> dict:
    seeds = jax.random.split(jax.random.key(seed), 5)
    field = bell_draw(seeds[0], (SAMPLES, NX, C, NY, NZ), 1.0, 6.0, ((0, 8), (1, 64)))
    cotangent = bell_draw(seeds[1], (SAMPLES, NX, C, NY, NZ), 1.0, 6.0, ((0, 8), (1, 64)))
    spectral_weight = bell_draw(seeds[2], (PAIRS, KX, 2 * C * C), 0.5, 3.0, ((0, 64),))
    pointwise_weight = bell_draw(seeds[3], (C, C), C ** -0.5, 1.0)
    return dict(field=field, cotangent=cotangent, spectral_weight=spectral_weight, pointwise_weight=pointwise_weight)


def kept_freqs(half_count, length):
    index_range = jnp.arange(2 * half_count, dtype=jnp.int32)
    return jnp.where(index_range < half_count, index_range, index_range + length - 2 * half_count).astype(jnp.int32)

def spectral(values, real_w, imag_w):
    freq_x = kept_freqs(MX, NX)
    freq_y = kept_freqs(M, NY)
    transform = jnp.fft.rfftn(values, axes=(0, 2, 3))
    picked = transform[freq_x][:, :, freq_y][:, :, :, :M]
    flattened = picked.reshape(KX, C, PAIRS)
    weight = lax.complex(real_w, imag_w)
    mixed = jnp.einsum('kiq,qkio->koq', flattened, weight)
    mode_block = mixed.reshape(KX, C, 2 * M, M)
    padded_rows = jnp.zeros((KX, C, NY, NZ // 2 + 1), transform.dtype).at[:, :, freq_y, :M].set(mode_block)
    spectrum = jnp.zeros((NX, C, NY, NZ // 2 + 1), transform.dtype).at[freq_x].set(padded_rows)
    return jnp.fft.irfftn(spectrum, s=(NX, NY, NZ), axes=(0, 2, 3))

def reference(field, cotangent, spectral_weight, pointwise_weight):
    weight = spectral_weight.astype(jnp.float32).reshape(PAIRS, KX, 2, C, C)
    real_w = weight[:, :, 0]
    imag_w = weight[:, :, 1]
    pointwise = pointwise_weight.astype(jnp.float32)
    field_grads = []
    total_real = jnp.zeros((PAIRS, KX, C, C), jnp.float32)
    total_imag = jnp.zeros((PAIRS, KX, C, C), jnp.float32)
    for sample in range(SAMPLES):
        values = field[sample].astype(jnp.float32)
        upstream = cotangent[sample].astype(jnp.float32)
        output_unused, pullback = jax.vjp(spectral, values, real_w, imag_w)
        d_values, d_real, d_imag = pullback(upstream)
        linear = jnp.einsum('pdyz,cd->pcyz', upstream, pointwise)
        field_grads.append((d_values + linear).astype(jnp.bfloat16))
        total_real = total_real + d_real
        total_imag = total_imag + d_imag
    weight_grad = jnp.stack([total_real, total_imag], axis=2).reshape(PAIRS, KX, 2 * C * C)
    return (jnp.stack(field_grads), weight_grad)
```

```python
import functools
import math

import jax
import jax.numpy as jnp
import ml_dtypes
import numpy as np
from jax import lax
from jax.experimental import pallas as pl
from jax.experimental.pallas import tpu as pltpu
from jax.sharding import PartitionSpec as P

MESH = pl.DeviceIdType.MESH
BF = jnp.bfloat16
F32 = jnp.float32
C = 32
M = 16
NY = NZ = 128
NX = 64
KX = 32
DP = 8
GX = 64
CELLS = NX * NY * NZ


def halves(table):
    high = table.astype(ml_dtypes.bfloat16)
    low = (table - high.astype(np.float64)).astype(ml_dtypes.bfloat16)
    return high, low


def angles(freqs, length):
    product = np.outer(freqs, np.arange(length)) % length
    return product * (2.0 * math.pi / length)


@functools.cache
def tables():
    freq_y = np.r_[0:M, NY - M : NY]
    freq_x = np.r_[0 : KX // 2, NX - KX // 2 : NX]
    freq_z = np.arange(M)
    ay, ax, az = angles(freq_y, NY), angles(freq_x, NX), angles(freq_z, NZ)

    def stack_rows(table):
        high, low = halves(table)
        return np.concatenate(
            [np.concatenate([high, high], 1), np.concatenate([low, np.zeros_like(low)], 1)], 0
        )

    def stack_three(table):
        high, low = halves(table)
        return np.concatenate([high, high, low], 1)

    fwd_y = np.concatenate(halves(np.concatenate([np.cos(ay), -np.sin(ay)])), 0)
    fwd_z = stack_rows(np.concatenate([np.cos(az), np.sin(az)]))
    fwd_x = stack_rows(np.concatenate([np.cos(ax), np.sin(ax)]))
    inv_x = stack_three(np.concatenate([np.cos(ax), np.sin(ax)]).T)
    inv_y = stack_three(np.concatenate([np.cos(ay), np.sin(ay)]).T)

    scale = np.ones((M, 2, 2, C), np.float32)
    scale[:, :, 1] = (np.where(freq_z == 0, 1.0, 2.0) / CELLS)[:, None, None]
    scale = scale.reshape(M, 128)

    wave = np.stack([np.cos(az), -np.sin(az)], 1).reshape(2, 8, 2, NZ)
    inv_z = np.zeros((2, 8, 8, 2, 8, NZ))
    for i in range(8):
        inv_z[:, i, :, :, i] = wave
    inv_z = np.concatenate(halves(inv_z.reshape(256, 1024)), 0)

    sums = np.zeros((8, 2, 8, C, 2, 8, 8, 2), np.float32)
    for q in range(8):
        for i in range(8):
            sums[q, 0, i, :, 0, i, q, 0] = 1
            sums[q, 1, i, :, 0, i, q, 1] = 1
            sums[q, 0, i, :, 1, i, q, 1] = 1
            sums[q, 1, i, :, 1, i, q, 0] = -1
    sums = sums.reshape(4096, 256).astype(ml_dtypes.bfloat16)

    spread_cot = np.zeros((2, 2, 2, C, 2, 4, C), np.float32)
    spread_in = np.zeros((8, 2, 2, 2, C, 2, 4, C), np.float32)
    for r in range(2):
        for o in range(C):
            spread_cot[:, r, 1, o, r, :, o] = 1
        for i in range(C):
            spread_in[i // 4, :, r, 0, i, r, i % 4, :] = 1
    spread_cot = spread_cot.reshape(256, 256).astype(ml_dtypes.bfloat16)
    spread_in = spread_in.reshape(8, 256, 256).astype(ml_dtypes.bfloat16)

    repeat16 = np.repeat(np.eye(C, dtype=np.float32), 16, 0).astype(ml_dtypes.bfloat16)
    small = [fwd_y, fwd_z, fwd_x, inv_x, inv_y, scale, spread_cot, repeat16]
    return small + [inv_z, sums, spread_in]


def split(value):
    high = value.astype(BF)
    return high, (value - high.astype(F32)).astype(BF)


def dot(left, right):
    return jnp.dot(left, right, preferred_element_type=F32)


def dot_nt(left, right):
    return lax.dot_general(left, right, (((1,), (1,)), ((), ())), preferred_element_type=F32)


def kernel(
    field_h, cot_h, weight_h, pw_ref,
    fwd_y, fwd_z, fwd_x, inv_x, inv_y, scale, spread_cot, repeat16,
    inv_z_h, sums_h, spread_in_h,
    out_ref, wg_ref,
    fx, cx, wv, inv_z, sums, spread_in,
    planes, send, recv, mb, wgr, prod, sb, rb, lin,
    load_sem, send_sem, recv_sem,
):
    dp = lax.axis_index("dp")
    me = lax.axis_index("gx")

    loads = []
    for n, (src, dst) in enumerate(((field_h, fx), (cot_h, cx))):
        for h in range(2):
            loads.append(pltpu.make_async_copy(
                src.at[0, 0, pl.ds(16 * h, 16)], dst.at[pl.ds(16 * h, 16)], load_sem.at[2 * n + h]
            ))
    later = [
        pltpu.make_async_copy(src, dst, load_sem.at[4 + n])
        for n, (src, dst) in enumerate(
            ((weight_h, wv), (sums_h, sums), (inv_z_h, inv_z), (spread_in_h, spread_in))
        )
    ]
    for copy in loads + later:
        copy.start()

    barrier = pltpu.get_barrier_semaphore()

    @pl.loop(1, GX)
    def _(step):
        pl.semaphore_signal(
            barrier, inc=1, device_id={"gx": lax.rem(me + step, GX)}, device_id_type=MESH
        )

    @pl.loop(1, DP)
    def _(step):
        pl.semaphore_signal(
            barrier, inc=1, device_id={"dp": lax.rem(dp + step, DP)}, device_id_type=MESH
        )

    lane = lax.broadcasted_iota(jnp.int32, (1, 128), 1)
    sign = jnp.where(lane < 64, 1.0, -1.0).astype(F32)
    odd = lax.rem(lane, 2) == 1

    for n, data in enumerate((fx, cx)):
        for h in range(2):
            loads[2 * n + h].wait()

            @pl.loop(0, 2)
            def _(step):
                for u in range(8):
                    c = 16 * h + 8 * step + u
                    along = dot(fwd_y[...], data[c])
                    planes[pl.ds(pl.multiple_of((32 * n + c) * 64, 64), 64), :] = (
                        along[:64] + along[64:]
                    )

    pl.semaphore_wait(barrier, GX - 1 + DP - 1)

    def send_copy(target):
        rows = pl.ds(pl.multiple_of(target * 8, 8), 8)
        return pltpu.make_async_remote_copy(
            src_ref=send.at[rows],
            dst_ref=recv.at[pl.ds(pl.multiple_of(me * 8, 8), 8)],
            send_sem=send_sem.at[0],
            recv_sem=recv_sem.at[0],
            device_id={"gx": target},
            device_id_type=MESH,
        )

    own = lax.div(me, 2)

    @pl.loop(0, 4)
    def _(step):
        for u in range(8):
            ky = lax.rem(own + 8 * step + u, 32)
            rows = jnp.concatenate(
                [planes[pl.ds(ky, 64, stride=64), :], planes[pl.ds(32 + ky, 64, stride=64), :]], 0
            )
            high, low = split(rows)
            modes = dot_nt(fwd_z[...], jnp.concatenate([high, low], 1))
            modes = modes[:32] + modes[32:]
            modes = (modes[:16] + sign * pltpu.roll(modes[16:], 64, 1)) * scale[...]
            send[pl.ds(pl.multiple_of(ky * 16, 16), 16), :] = modes
        for u in range(16):
            target = lax.rem(2 * own + 16 * step + u, GX)

            @pl.when(target != me)
            def _():
                send_copy(target).start()

    mine = pl.ds(pl.multiple_of(me * 8, 8), 8)
    recv[mine, :] = send[mine, :]

    pw_rows = dot(repeat16[...], pw_ref[...]).astype(BF)
    kron = dot_nt(pw_rows, repeat16[...])
    rows_i = lax.broadcasted_iota(jnp.int32, (512, 512), 0)
    cols_i = lax.broadcasted_iota(jnp.int32, (512, 512), 1)
    kron = jnp.where(lax.rem(rows_i, 16) == lax.rem(cols_i, 16), kron, 0.0).astype(BF)
    for g in range(8):
        block = cx[:, 16 * g : 16 * g + 16, :].reshape(512, 128)
        lin[:, 16 * g : 16 * g + 16, :] = dot(kron, block).reshape(32, 16, 128)

    def drain(buffer, rows, index):
        return pltpu.make_async_remote_copy(
            src_ref=buffer[0].at[rows], dst_ref=buffer[1].at[rows],
            send_sem=send_sem.at[index], recv_sem=recv_sem.at[index],
            device_id={"gx": lax.rem(me + 1, GX)}, device_id_type=MESH,
        )

    first = drain((send, recv), pl.ds(0, 504), 0)
    first.wait_recv()

    cols = []
    for q in range(8):
        high, low = split(recv[pl.ds(q, 64, stride=8), :])
        cols.append(jnp.concatenate([high, low], 0))
    modes_x = dot(fwd_x[...], jnp.concatenate(cols, 1))
    modes_x = modes_x[:64] + modes_x[64:]
    modes = []
    for q in range(8):
        part = modes_x[:, 128 * q : 128 * q + 128]
        part = part[:32] + sign * pltpu.roll(part[32:], 64, 1)
        mb[pl.ds(q, 32, stride=8), :] = part
        modes.append(part)

    def dp_copy(target):
        return pltpu.make_async_remote_copy(
            src_ref=mb.at[pl.ds(pl.multiple_of(target * 32, 32), 32)],
            dst_ref=wgr.at[pl.ds(pl.multiple_of(dp * 32, 32), 32)],
            send_sem=send_sem.at[1],
            recv_sem=recv_sem.at[1],
            device_id={"dp": target},
            device_id_type=MESH,
        )

    @pl.loop(1, DP)
    def _(step):
        dp_copy(lax.rem(dp + step, DP)).start()

    ours = pl.ds(pl.multiple_of(dp * 32, 32), 32)
    wgr[ours, :] = mb[ours, :]

    for copy in later[:2]:
        copy.wait()
    high, low = split(jnp.concatenate(modes, 0))
    spread = dot(jnp.concatenate([high, low], 1), spread_cot[...])
    for q in range(8):
        cr = spread[32 * q : 32 * q + 32, :128]
        ci = spread[32 * q : 32 * q + 32, 128:]
        for a in range(4):
            for g in range(2):
                col = 256 * a + 128 * g
                wr = wv[q, :, col : col + 128].astype(F32)
                wi = wv[q, :, 1024 + col : 1024 + col + 128].astype(F32)
                for r, value in enumerate((cr * wr + ci * wi, ci * wr - cr * wi)):
                    high, low = split(value)
                    at = 512 * q + 256 * r + 128 * g
                    prod[32 * a : 32 * a + 32, at : at + 128] = high
                    prod[128 + 32 * a : 160 + 32 * a, at : at + 128] = low
    grad = dot(prod[...], sums[...])
    grad = grad[:128] + grad[128:]
    pieces = [
        jnp.concatenate([grad[32 * a : 32 * a + 32, :128], grad[32 * a : 32 * a + 32, 128:]], 0)
        for a in range(4)
    ]
    high, low = split(jnp.concatenate(pieces, 1))
    back = dot(inv_x[...], jnp.concatenate([high, low, high], 0))
    for a in range(4):
        sb[pl.ds(a, 64, stride=4), :] = back[:, 128 * a : 128 * a + 128]

    sb3 = sb.reshape(64, 4, 128)
    rb3 = rb.reshape(64, 4, 128)

    def back_copy(target):
        return pltpu.make_async_remote_copy(
            src_ref=sb3.at[target],
            dst_ref=rb3.at[me],
            send_sem=send_sem.at[2],
            recv_sem=recv_sem.at[2],
            device_id={"gx": target},
            device_id_type=MESH,
        )

    @pl.loop(1, GX)
    def _(step):
        back_copy(lax.rem(me + step, GX)).start()

    rb3[me] = sb3[me]

    dp_drain = pltpu.make_async_remote_copy(
        src_ref=mb.at[pl.ds(0, 224)], dst_ref=wgr.at[pl.ds(0, 224)],
        send_sem=send_sem.at[1], recv_sem=recv_sem.at[1],
        device_id={"dp": lax.rem(dp + 1, DP)}, device_id_type=MESH,
    )
    later[3].wait()
    dp_drain.wait_recv()
    high, low = split(wgr[...])
    pair = jnp.concatenate([high, low], 1)
    spread = dot(pair, spread_cot[...])
    cr = spread[:, :128]
    ci = spread[:, 128:]
    for j in range(8):
        inner = dot(pair, spread_in[j])
        ir = inner[:, :128]
        ii = inner[:, 128:]
        for r, value in enumerate((ir * cr + ii * ci, ir * ci - ii * cr)):
            total = value[0:32]
            for s in range(1, 8):
                total = total + value[32 * s : 32 * s + 32]
            at = 1024 * r + 128 * j
            wg_ref[:, :, at : at + 128] = total.reshape(4, 8, 128)

    later[2].wait()
    third = drain((sb, rb), pl.ds(0, 252), 2)
    third.wait_recv()
    tops, bottoms = [], []
    for n in range(8):
        value = rb[pl.ds(n, 32, stride=8), :]
        tops.append(value)
        bottoms.append(jnp.where(odd, pltpu.roll(value, 1, 1), -pltpu.roll(value, 127, 1)))
    stacked = jnp.concatenate([jnp.concatenate(tops, 1), jnp.concatenate(bottoms, 1)], 0)
    high, low = split(stacked)
    along = dot(inv_y[...], jnp.concatenate([high, low, high], 0))
    for a in range(4):
        value = jnp.concatenate(
            [along[:, 128 * a : 128 * a + 128], along[:, 512 + 128 * a : 640 + 128 * a]], 1
        )
        high, low = split(value)
        both = jnp.concatenate([high, low], 0)
        for n in range(4):
            part = dot(both, inv_z[:256, 256 * n : 256 * n + 256])
            total = part[:128] + part[128:] + dot(high, inv_z[256:, 256 * n : 256 * n + 256])
            for u in range(2):
                c = 8 * a + 2 * n + u
                out_ref[0, 0, c] = (total[:, 128 * u : 128 * u + 128] + lin[c]).astype(BF)

    first.wait_send()
    dp_drain.wait_send()
    third.wait_send()


def on_device(field, cotangent, spectral_weight, pointwise_weight):
    consts = [jnp.asarray(table) for table in tables()]
    hbm = pl.BlockSpec(memory_space=pltpu.HBM)
    vmem = pl.BlockSpec(memory_space=pltpu.VMEM)
    field_grad, weight_grad = pl.pallas_call(
        kernel,
        out_shape=(
            jax.ShapeDtypeStruct((1, 1, C, NY, NZ), BF),
            jax.ShapeDtypeStruct((4, 8, 2 * C * C), F32),
        ),
        in_specs=[hbm, hbm, hbm, vmem] + [vmem] * 8 + [hbm] * 3,
        out_specs=(vmem, vmem),
        scratch_shapes=[
            pltpu.VMEM((C, NY, NZ), BF),
            pltpu.VMEM((C, NY, NZ), BF),
            pltpu.VMEM((8, KX, 2 * C * C), BF),
            pltpu.VMEM((512, 1024), BF),
            pltpu.VMEM((4096, 256), BF),
            pltpu.VMEM((8, 256, 256), BF),
            pltpu.VMEM((4096, 128), F32),
            pltpu.VMEM((512, 128), F32),
            pltpu.VMEM((512, 128), F32),
            pltpu.VMEM((256, 128), F32),
            pltpu.VMEM((256, 128), F32),
            pltpu.VMEM((256, 4096), BF),
            pltpu.VMEM((256, 128), F32),
            pltpu.VMEM((256, 128), F32),
            pltpu.VMEM((C, NY, NZ), F32),
            pltpu.SemaphoreType.DMA((8,)),
            pltpu.SemaphoreType.DMA((3,)),
            pltpu.SemaphoreType.DMA((3,)),
        ],
        compiler_params=pltpu.CompilerParams(
            collective_id=0, has_side_effects=True, vmem_limit_bytes=48 << 20
        ),
        cost_estimate=pl.CostEstimate(flops=10**10, bytes_accessed=10**7, transcendentals=0),
    )(field, cotangent, spectral_weight, pointwise_weight, *consts)
    return field_grad, jnp.transpose(weight_grad, (1, 0, 2))


def solution(mesh):
    placed = (
        P("dp", "gx", None, None, None),
        P("dp", "gx", None, None, None),
        P("gx", None, None),
        P(),
    )
    return jax.shard_map(
        on_device,
        mesh=mesh,
        in_specs=placed,
        out_specs=(P("dp", "gx", None, None, None), P("gx", "dp", None)),
        check_vma=False,
    )
```

```python
import functools
import math

import jax
import jax.numpy as jnp
import ml_dtypes
import numpy as np
from jax import lax
from jax.experimental import pallas as pl
from jax.experimental.pallas import tpu as pltpu
from jax.sharding import PartitionSpec as P

MESH = pl.DeviceIdType.MESH
BF = jnp.bfloat16
F32 = jnp.float32
C = 32
M = 16
NY = NZ = 128
NX = 64
KX = 32
DP = 8
GX = 64
CELLS = NX * NY * NZ


def halves(table):
    high = table.astype(ml_dtypes.bfloat16)
    low = (table - high.astype(np.float64)).astype(ml_dtypes.bfloat16)
    return high, low


def angles(freqs, length):
    product = np.outer(freqs, np.arange(length)) % length
    return product * (2.0 * math.pi / length)


@functools.cache
def tables():
    freq_y = np.r_[0:M, NY - M : NY]
    freq_x = np.r_[0 : KX // 2, NX - KX // 2 : NX]
    freq_z = np.arange(M)
    ay, ax, az = angles(freq_y, NY), angles(freq_x, NX), angles(freq_z, NZ)

    def stack_rows(table):
        high, low = halves(table)
        return np.concatenate(
            [np.concatenate([high, high], 1), np.concatenate([low, np.zeros_like(low)], 1)], 0
        )

    def stack_three(table):
        high, low = halves(table)
        return np.concatenate([high, high, low], 1)

    fwd_y = np.concatenate(halves(np.concatenate([np.cos(ay), -np.sin(ay)])), 0)
    fwd_z = stack_rows(np.concatenate([np.cos(az), np.sin(az)]))
    fwd_x = stack_rows(np.concatenate([np.cos(ax), np.sin(ax)]))
    inv_x = stack_three(np.concatenate([np.cos(ax), np.sin(ax)]).T)
    inv_y = stack_three(np.concatenate([np.cos(ay), np.sin(ay)]).T)

    wave = np.stack([np.cos(az), -np.sin(az)], 1).reshape(2, 8, 2, NZ)
    inv_z = np.zeros((2, 8, 8, 2, 8, NZ))
    for i in range(8):
        inv_z[:, i, :, :, i] = wave
    inv_z = np.concatenate(halves(inv_z.reshape(256, 1024)), 0)

    sums = np.zeros((8, 2, 8, C, 2, 8, 8, 2), np.float32)
    for q in range(8):
        for i in range(8):
            sums[q, 0, i, :, 0, i, q, 0] = 1
            sums[q, 1, i, :, 0, i, q, 1] = 1
            sums[q, 0, i, :, 1, i, q, 1] = 1
            sums[q, 1, i, :, 1, i, q, 0] = -1
    sums = sums.reshape(4096, 256).astype(ml_dtypes.bfloat16)

    spread_cot = np.zeros((2, 2, 2, C, 2, 4, C), np.float32)
    spread_in = np.zeros((8, 2, 2, 2, C, 2, 4, C), np.float32)
    for r in range(2):
        for o in range(C):
            spread_cot[:, r, 1, o, r, :, o] = 1
        for i in range(C):
            spread_in[i // 4, :, r, 0, i, r, i % 4, :] = 1
    spread_cot = spread_cot.reshape(256, 256).astype(ml_dtypes.bfloat16)
    spread_in = spread_in.reshape(8, 256, 256).astype(ml_dtypes.bfloat16)

    def widen(table):
        return np.pad(table, ((0, 0), (0, 256 - table.shape[1])))

    small = np.concatenate(
        [np.concatenate([fwd_y, fwd_x], 1), fwd_z, widen(inv_x), widen(inv_y), spread_cot], 0
    )
    return small, inv_z, sums, spread_in


def split(value):
    high = value.astype(BF)
    return high, (value - high.astype(F32)).astype(BF)


def dot(left, right):
    return jnp.dot(left, right, preferred_element_type=F32)


def dot_nt(left, right):
    return lax.dot_general(left, right, (((1,), (1,)), ((), ())), preferred_element_type=F32)


def far_first(me, step):
    y, x, z = lax.div(me, 8), lax.rem(lax.div(me, 2), 4), lax.rem(me, 2)
    dz = 1 - lax.div(step, 32)
    ky = far_pair(y, x, lax.rem(step, 32))
    return 2 * ky + lax.rem(z + dz, 2)


def far_pair(y, x, step):
    m, j = lax.div(step, 4), lax.rem(step, 4)
    half = lax.div(m + 1, 2)
    dy = jnp.where(lax.rem(m, 2) == 0, 4 + half, 4 - half)
    dx = jnp.where(j == 3, 0, jnp.where(j == 2, 3, 2 - j))
    return lax.rem(y + dy, 8) * 4 + lax.rem(x + dx, 4)


def kernel(
    field_h, cot_h, weight_h, pw_h, small_h, inv_z_h, sums_h, spread_in_h,
    out_ref, wg_ref,
    fx, cx, wv, pw, small, inv_z, sums, spread_in,
    planes, send, recv, mb, wgr, prod, sb, rb, lin,
    load_sem, send_sem, recv_sem,
):
    dp = lax.axis_index("dp")
    me = lax.axis_index("gx")

    loads = []
    for n, (src, dst) in enumerate(((field_h, fx), (cot_h, cx))):
        for h in range(2):
            loads.append(pltpu.make_async_copy(
                src.at[0, 0, pl.ds(16 * h, 16)], dst.at[pl.ds(16 * h, 16)], load_sem.at[2 * n + h]
            ))
    later = [
        pltpu.make_async_copy(src, dst, load_sem.at[4 + n])
        for n, (src, dst) in enumerate(
            ((weight_h, wv), (sums_h, sums), (inv_z_h, inv_z), (spread_in_h, spread_in), (pw_h, pw))
        )
    ]
    table_load = pltpu.make_async_copy(small_h, small, load_sem.at[9])
    for copy in [table_load] + loads:
        copy.start()
    fwd_y = small.at[0:128, 0:128]
    fwd_x = small.at[0:128, 128:256]
    fwd_z = small.at[128:192]
    inv_x = small.at[192:256, 0:192]
    inv_y = small.at[256:384, 0:192]
    spread_cot = small.at[384:640]

    barrier = pltpu.get_barrier_semaphore()

    @pl.loop(0, GX - 1)
    def _(step):
        pl.semaphore_signal(
            barrier, inc=1, device_id={"gx": far_first(me, step)}, device_id_type=MESH
        )

    @pl.loop(1, DP)
    def _(step):
        pl.semaphore_signal(
            barrier, inc=1, device_id={"dp": lax.rem(dp + step, DP)}, device_id_type=MESH
        )

    lane = lax.broadcasted_iota(jnp.int32, (1, 128), 1)
    sign = jnp.where(lane < 64, 1.0, -1.0).astype(F32)
    odd = lax.rem(lane, 2) == 1
    kz = lax.broadcasted_iota(jnp.int32, (M, 128), 0)
    scale = jnp.where(
        lax.rem(lane, 64) < 32, 1.0, jnp.where(kz == 0, 1.0 / CELLS, 2.0 / CELLS)
    ).astype(F32)
    repeat_row = lax.div(lax.broadcasted_iota(jnp.int32, (512, C), 0), 16)
    repeat_col = lax.broadcasted_iota(jnp.int32, (512, C), 1)
    repeat16 = jnp.where(repeat_row == repeat_col, 1.0, 0.0).astype(BF)

    table_load.wait()

    for n, data in enumerate((fx, cx)):
        for h in range(2):
            loads[2 * n + h].wait()

            @pl.loop(0, 2)
            def _(step):
                for u in range(8):
                    c = 16 * h + 8 * step + u
                    along = dot(fwd_y[...], data[c])
                    planes[pl.ds(pl.multiple_of((32 * n + c) * 64, 64), 64), :] = (
                        along[:64] + along[64:]
                    )

    for copy in later:
        copy.start()

    def send_copy(target):
        rows = pl.ds(pl.multiple_of(target * 8, 8), 8)
        return pltpu.make_async_remote_copy(
            src_ref=send.at[rows],
            dst_ref=recv.at[pl.ds(pl.multiple_of(me * 8, 8), 8)],
            send_sem=send_sem.at[0],
            recv_sem=recv_sem.at[0],
            device_id={"gx": target},
            device_id_type=MESH,
        )

    @pl.loop(0, 4)
    def _(step):
        for u in range(8):
            ky = 8 * step + u
            rows = jnp.concatenate(
                [planes[pl.ds(ky, 64, stride=64), :], planes[pl.ds(32 + ky, 64, stride=64), :]], 0
            )
            high, low = split(rows)
            modes = dot_nt(fwd_z[...], jnp.concatenate([high, low], 1))
            modes = modes[:32] + modes[32:]
            modes = (modes[:16] + sign * pltpu.roll(modes[16:], 64, 1)) * scale
            send[pl.ds(pl.multiple_of(ky * 16, 16), 16), :] = modes

    pl.semaphore_wait(barrier, GX - 1 + DP - 1)

    @pl.loop(0, GX - 1)
    def _(step):
        send_copy(far_first(me, step)).start()

    mine = pl.ds(pl.multiple_of(me * 8, 8), 8)
    recv[mine, :] = send[mine, :]

    later[4].wait()
    pw_rows = dot(repeat16, pw[...]).astype(BF)
    kron = dot_nt(pw_rows, repeat16)
    rows_i = lax.broadcasted_iota(jnp.int32, (512, 512), 0)
    cols_i = lax.broadcasted_iota(jnp.int32, (512, 512), 1)
    kron = jnp.where(lax.rem(rows_i, 16) == lax.rem(cols_i, 16), kron, 0.0).astype(BF)
    for g in range(8):
        block = cx[:, 16 * g : 16 * g + 16, :].reshape(512, 128)
        lin[:, 16 * g : 16 * g + 16, :] = dot(kron, block).reshape(32, 16, 128)

    def drain(buffer, rows, index):
        return pltpu.make_async_remote_copy(
            src_ref=buffer[0].at[rows], dst_ref=buffer[1].at[rows],
            send_sem=send_sem.at[index], recv_sem=recv_sem.at[index],
            device_id={"gx": lax.rem(me + 1, GX)}, device_id_type=MESH,
        )

    first = drain((send, recv), pl.ds(0, 504), 0)
    first.wait_recv()

    cols = []
    for q in range(8):
        high, low = split(recv[pl.ds(q, 64, stride=8), :])
        cols.append(jnp.concatenate([high, low], 0))
    modes_x = dot(fwd_x[...], jnp.concatenate(cols, 1))
    modes_x = modes_x[:64] + modes_x[64:]
    modes = []
    for q in range(8):
        part = modes_x[:, 128 * q : 128 * q + 128]
        part = part[:32] + sign * pltpu.roll(part[32:], 64, 1)
        mb[pl.ds(q, 32, stride=8), :] = part
        modes.append(part)

    def dp_copy(target):
        return pltpu.make_async_remote_copy(
            src_ref=mb.at[pl.ds(pl.multiple_of(target * 32, 32), 32)],
            dst_ref=wgr.at[pl.ds(pl.multiple_of(dp * 32, 32), 32)],
            send_sem=send_sem.at[1],
            recv_sem=recv_sem.at[1],
            device_id={"dp": target},
            device_id_type=MESH,
        )

    @pl.loop(1, DP)
    def _(step):
        dp_copy(lax.rem(dp + step, DP)).start()

    ours = pl.ds(pl.multiple_of(dp * 32, 32), 32)
    wgr[ours, :] = mb[ours, :]

    for copy in later[:2]:
        copy.wait()
    high, low = split(jnp.concatenate(modes, 0))
    spread = dot(jnp.concatenate([high, low], 1), spread_cot[...])
    for q in range(8):
        cr = spread[32 * q : 32 * q + 32, :128]
        ci = spread[32 * q : 32 * q + 32, 128:]
        for a in range(4):
            for g in range(2):
                col = 256 * a + 128 * g
                wr = wv[q, :, col : col + 128].astype(F32)
                wi = wv[q, :, 1024 + col : 1024 + col + 128].astype(F32)
                for r, value in enumerate((cr * wr + ci * wi, ci * wr - cr * wi)):
                    high, low = split(value)
                    at = 512 * q + 256 * r + 128 * g
                    prod[32 * a : 32 * a + 32, at : at + 128] = high
                    prod[128 + 32 * a : 160 + 32 * a, at : at + 128] = low
    grad = dot(prod[...], sums[...])
    grad = grad[:128] + grad[128:]
    pieces = [
        jnp.concatenate([grad[32 * a : 32 * a + 32, :128], grad[32 * a : 32 * a + 32, 128:]], 0)
        for a in range(4)
    ]
    high, low = split(jnp.concatenate(pieces, 1))
    back = dot(inv_x[...], jnp.concatenate([high, low, high], 0))
    for a in range(4):
        sb[pl.ds(a, 64, stride=4), :] = back[:, 128 * a : 128 * a + 128]

    sb3 = sb.reshape(64, 4, 128)
    rb3 = rb.reshape(64, 4, 128)

    def back_copy(target):
        return pltpu.make_async_remote_copy(
            src_ref=sb3.at[target],
            dst_ref=rb3.at[me],
            send_sem=send_sem.at[2],
            recv_sem=recv_sem.at[2],
            device_id={"gx": target},
            device_id_type=MESH,
        )

    @pl.loop(0, GX - 1)
    def _(step):
        back_copy(far_first(me, step)).start()

    rb3[me] = sb3[me]

    dp_drain = pltpu.make_async_remote_copy(
        src_ref=mb.at[pl.ds(0, 224)], dst_ref=wgr.at[pl.ds(0, 224)],
        send_sem=send_sem.at[1], recv_sem=recv_sem.at[1],
        device_id={"dp": lax.rem(dp + 1, DP)}, device_id_type=MESH,
    )
    later[3].wait()
    dp_drain.wait_recv()
    high, low = split(wgr[...])
    pair = jnp.concatenate([high, low], 1)
    spread = dot(pair, spread_cot[...])
    cr = spread[:, :128]
    ci = spread[:, 128:]
    for j in range(8):
        inner = dot(pair, spread_in[j])
        ir = inner[:, :128]
        ii = inner[:, 128:]
        for r, value in enumerate((ir * cr + ii * ci, ir * ci - ii * cr)):
            total = value[0:32]
            for s in range(1, 8):
                total = total + value[32 * s : 32 * s + 32]
            at = 1024 * r + 128 * j
            wg_ref[:, :, at : at + 128] = total.reshape(4, 8, 128)

    later[2].wait()
    third = drain((sb, rb), pl.ds(0, 252), 2)
    third.wait_recv()
    tops, bottoms = [], []
    for n in range(8):
        value = rb[pl.ds(n, 32, stride=8), :]
        tops.append(value)
        bottoms.append(jnp.where(odd, pltpu.roll(value, 1, 1), -pltpu.roll(value, 127, 1)))
    stacked = jnp.concatenate([jnp.concatenate(tops, 1), jnp.concatenate(bottoms, 1)], 0)
    high, low = split(stacked)
    along = dot(inv_y[...], jnp.concatenate([high, low, high], 0))
    for a in range(4):
        value = jnp.concatenate(
            [along[:, 128 * a : 128 * a + 128], along[:, 512 + 128 * a : 640 + 128 * a]], 1
        )
        high, low = split(value)
        both = jnp.concatenate([high, low], 0)
        for n in range(4):
            part = dot(both, inv_z[:256, 256 * n : 256 * n + 256])
            total = part[:128] + part[128:] + dot(high, inv_z[256:, 256 * n : 256 * n + 256])
            for u in range(2):
                c = 8 * a + 2 * n + u
                out_ref[0, 0, c] = (total[:, 128 * u : 128 * u + 128] + lin[c]).astype(BF)

    first.wait_send()
    dp_drain.wait_send()
    third.wait_send()


def on_device(field, cotangent, spectral_weight, pointwise_weight):
    consts = [jnp.asarray(table) for table in tables()]
    operands = [field, cotangent, spectral_weight, pointwise_weight, *consts]
    hbm = pl.BlockSpec(memory_space=pltpu.HBM)
    vmem = pl.BlockSpec(memory_space=pltpu.VMEM)
    field_grad, weight_grad = pl.pallas_call(
        kernel,
        out_shape=(
            jax.ShapeDtypeStruct((1, 1, C, NY, NZ), BF),
            jax.ShapeDtypeStruct((4, 8, 2 * C * C), F32),
        ),
        in_specs=[hbm] * 8,
        out_specs=(vmem, vmem),
        scratch_shapes=[
            pltpu.VMEM((C, NY, NZ), BF),
            pltpu.VMEM((C, NY, NZ), BF),
            pltpu.VMEM((8, KX, 2 * C * C), BF),
            pltpu.VMEM((C, C), BF),
            pltpu.VMEM((640, 256), BF),
            pltpu.VMEM((512, 1024), BF),
            pltpu.VMEM((4096, 256), BF),
            pltpu.VMEM((8, 256, 256), BF),
            pltpu.VMEM((4096, 128), F32),
            pltpu.VMEM((512, 128), F32),
            pltpu.VMEM((512, 128), F32),
            pltpu.VMEM((256, 128), F32),
            pltpu.VMEM((256, 128), F32),
            pltpu.VMEM((256, 4096), BF),
            pltpu.VMEM((256, 128), F32),
            pltpu.VMEM((256, 128), F32),
            pltpu.VMEM((C, NY, NZ), F32),
            pltpu.SemaphoreType.DMA((10,)),
            pltpu.SemaphoreType.DMA((3,)),
            pltpu.SemaphoreType.DMA((3,)),
        ],
        compiler_params=pltpu.CompilerParams(
            collective_id=0, has_side_effects=True, vmem_limit_bytes=48 << 20
        ),
        cost_estimate=pl.CostEstimate(flops=10**10, bytes_accessed=10**7, transcendentals=0),
    )(*[pltpu.with_memory_space_constraint(x, pltpu.HBM) for x in operands])
    return field_grad, jnp.transpose(weight_grad, (1, 0, 2))


def solution(mesh):
    placed = (
        P("dp", "gx", None, None, None),
        P("dp", "gx", None, None, None),
        P("gx", None, None),
        P(),
    )
    return jax.shard_map(
        on_device,
        mesh=mesh,
        in_specs=placed,
        out_specs=(P("dp", "gx", None, None, None), P("gx", "dp", None)),
        check_vma=False,
    )
```

```python
import functools
import math

import jax
import jax.numpy as jnp
import ml_dtypes
import numpy as np
from jax import lax
from jax.experimental import pallas as pl
from jax.experimental.pallas import tpu as pltpu
from jax.sharding import PartitionSpec as P

MESH = pl.DeviceIdType.MESH
BF = jnp.bfloat16
F32 = jnp.float32
C = 32
M = 16
NY = NZ = 128
NX = 64
KX = 32
DP = 8
GX = 64
PLANE = 32
CELLS = NX * NY * NZ


def halves(table):
    high = table.astype(ml_dtypes.bfloat16)
    low = (table - high.astype(np.float64)).astype(ml_dtypes.bfloat16)
    return high, low


def angles(freqs, length):
    product = np.outer(freqs, np.arange(length)) % length
    return product * (2.0 * math.pi / length)


@functools.cache
def tables():
    freq_y = np.r_[0:M, NY - M : NY]
    freq_x = np.r_[0 : KX // 2, NX - KX // 2 : NX]
    freq_z = np.arange(M)
    ay, ax, az = angles(freq_y, NY), angles(freq_x, NX), angles(freq_z, NZ)

    def stack_rows(table):
        high, low = halves(table)
        return np.concatenate(
            [np.concatenate([high, high], 1), np.concatenate([low, np.zeros_like(low)], 1)], 0
        )

    def stack_three(table):
        high, low = halves(table)
        return np.concatenate([high, high, low], 1)

    fwd_y = np.concatenate(halves(np.concatenate([np.cos(ay), -np.sin(ay)])), 0)
    fwd_z = stack_rows(np.concatenate([np.cos(az), np.sin(az)]))
    fwd_x = stack_rows(np.concatenate([np.cos(ax), np.sin(ax)]))
    inv_x = stack_three(np.concatenate([np.cos(ax), np.sin(ax)]).T)
    inv_y = stack_three(np.concatenate([np.cos(ay), np.sin(ay)]).T)

    wave = np.stack([np.cos(az), -np.sin(az)], 1).reshape(2, 8, 2, NZ)
    inv_z = np.zeros((2, 8, 8, 2, 8, NZ))
    for i in range(8):
        inv_z[:, i, :, :, i] = wave
    inv_z = np.concatenate(halves(inv_z.reshape(256, 1024)), 0)

    sums = np.zeros((8, 2, 8, C, 2, 8, 8, 2), np.float32)
    for q in range(8):
        for i in range(8):
            sums[q, 0, i, :, 0, i, q, 0] = 1
            sums[q, 1, i, :, 0, i, q, 1] = 1
            sums[q, 0, i, :, 1, i, q, 1] = 1
            sums[q, 1, i, :, 1, i, q, 0] = -1
    sums = sums.reshape(4096, 256).astype(ml_dtypes.bfloat16)

    spread_cot = np.zeros((2, 2, 2, C, 2, 4, C), np.float32)
    spread_in = np.zeros((8, 2, 2, 2, C, 2, 4, C), np.float32)
    for r in range(2):
        for o in range(C):
            spread_cot[:, r, 1, o, r, :, o] = 1
        for i in range(C):
            spread_in[i // 4, :, r, 0, i, r, i % 4, :] = 1
    spread_cot = spread_cot.reshape(256, 256).astype(ml_dtypes.bfloat16)
    spread_in = spread_in.reshape(8, 256, 256).astype(ml_dtypes.bfloat16)

    def widen(table):
        return np.pad(table, ((0, 0), (0, 256 - table.shape[1])))

    small = np.concatenate(
        [np.concatenate([fwd_y, fwd_x], 1), fwd_z, widen(inv_x), widen(inv_y), spread_cot], 0
    )
    return small, inv_z, sums, spread_in


def split(value):
    high = value.astype(BF)
    return high, (value - high.astype(F32)).astype(BF)


def dot(left, right):
    return jnp.dot(left, right, preferred_element_type=F32)


def dot_nt(left, right):
    return lax.dot_general(left, right, (((1,), (1,)), ((), ())), preferred_element_type=F32)


def far_first(me, step):
    y, x, z = lax.div(me, 8), lax.rem(lax.div(me, 2), 4), lax.rem(me, 2)
    dz = 1 - lax.div(step, 32)
    ky = far_pair(y, x, lax.rem(step, 32))
    return 2 * ky + lax.rem(z + dz, 2)


def far_pair(y, x, step):
    m, j = lax.div(step, 4), lax.rem(step, 4)
    half = lax.div(m + 1, 2)
    dy = jnp.where(lax.rem(m, 2) == 0, 4 + half, 4 - half)
    dx = jnp.where(j == 3, 0, jnp.where(j == 2, 3, 2 - j))
    return lax.rem(y + dy, 8) * 4 + lax.rem(x + dx, 4)


def kernel(
    field_h, cot_h, weight_h, pw_h, small_h, inv_z_h, sums_h, spread_in_h,
    out_ref, wg_ref,
    fx, cx, wv, pw, small, inv_z, sums, spread_in,
    planes, zout, send, recv, mb, wgr, prod, sb, rb, lin,
    load_sem, send_sem, recv_sem,
):
    dp = lax.axis_index("dp")
    me = lax.axis_index("gx")
    y, x, z = lax.div(me, 8), lax.rem(lax.div(me, 2), 4), lax.rem(me, 2)
    across = me + 1 - 2 * z
    place = lax.div(me, 2)

    loads = []
    for n, (src, dst) in enumerate(((field_h, fx), (cot_h, cx))):
        for h in range(2):
            loads.append(pltpu.make_async_copy(
                src.at[0, 0, pl.ds(16 * h, 16)], dst.at[pl.ds(16 * h, 16)], load_sem.at[2 * n + h]
            ))
    later = [
        pltpu.make_async_copy(src, dst, load_sem.at[4 + n])
        for n, (src, dst) in enumerate(
            ((weight_h, wv), (sums_h, sums), (inv_z_h, inv_z), (spread_in_h, spread_in), (pw_h, pw))
        )
    ]
    table_load = pltpu.make_async_copy(small_h, small, load_sem.at[9])
    for copy in [table_load] + loads:
        copy.start()
    fwd_y = small.at[0:128, 0:128]
    fwd_x = small.at[0:128, 128:256]
    fwd_z = small.at[128:192]
    inv_x = small.at[192:256, 0:192]
    inv_y = small.at[256:384, 0:192]
    spread_cot = small.at[384:640]

    barrier = pltpu.get_barrier_semaphore()

    @pl.loop(0, PLANE - 1)
    def _(step):
        pl.semaphore_signal(
            barrier, inc=1, device_id={"gx": 2 * far_pair(y, x, step) + z}, device_id_type=MESH
        )

    pl.semaphore_signal(barrier, inc=1, device_id={"gx": across}, device_id_type=MESH)

    @pl.loop(1, DP)
    def _(step):
        pl.semaphore_signal(
            barrier, inc=1, device_id={"dp": lax.rem(dp + step, DP)}, device_id_type=MESH
        )

    lane = lax.broadcasted_iota(jnp.int32, (1, 128), 1)
    sign = jnp.where(lane < 64, 1.0, -1.0).astype(F32)
    odd = lax.rem(lane, 2) == 1
    kz = lax.broadcasted_iota(jnp.int32, (M, 128), 0)
    scale = jnp.where(
        lax.rem(lane, 64) < 32, 1.0, jnp.where(kz == 0, 1.0 / CELLS, 2.0 / CELLS)
    ).astype(F32)
    repeat_row = lax.div(lax.broadcasted_iota(jnp.int32, (512, C), 0), 16)
    repeat_col = lax.broadcasted_iota(jnp.int32, (512, C), 1)
    repeat16 = jnp.where(repeat_row == repeat_col, 1.0, 0.0).astype(BF)

    table_load.wait()

    for n, data in enumerate((fx, cx)):
        for h in range(2):
            loads[2 * n + h].wait()

            @pl.loop(0, 2)
            def _(step):
                for u in range(8):
                    c = 16 * h + 8 * step + u
                    along = dot(fwd_y[...], data[c])
                    planes[pl.ds(pl.multiple_of((32 * n + c) * 64, 64), 64), :] = (
                        along[:64] + along[64:]
                    )

    for copy in later:
        copy.start()

    send4 = send.reshape(32, 2, 8, 128)
    zout3 = zout.reshape(32, 8, 128)

    def z_copy(part):
        rows = pl.ds(8 * part, 8)
        return pltpu.make_async_remote_copy(
            src_ref=zout3.at[rows],
            dst_ref=send4.at[rows, z],
            send_sem=send_sem.at[3],
            recv_sem=recv_sem.at[3],
            device_id={"gx": across},
            device_id_type=MESH,
        )

    def send_copy(target):
        return pltpu.make_async_remote_copy(
            src_ref=send.at[pl.ds(pl.multiple_of(target * 16, 16), 16)],
            dst_ref=recv.at[pl.ds(pl.multiple_of(place * 16, 16), 16)],
            send_sem=send_sem.at[0],
            recv_sem=recv_sem.at[0],
            device_id={"gx": 2 * target + z},
            device_id_type=MESH,
        )

    @pl.loop(0, 4)
    def _(step):
        for u in range(8):
            ky = 8 * step + u
            rows = jnp.concatenate(
                [planes[pl.ds(ky, 64, stride=64), :], planes[pl.ds(32 + ky, 64, stride=64), :]], 0
            )
            high, low = split(rows)
            modes = dot_nt(fwd_z[...], jnp.concatenate([high, low], 1))
            modes = modes[:32] + modes[32:]
            modes = (modes[:16] + sign * pltpu.roll(modes[16:], 64, 1)) * scale
            send[pl.ds(pl.multiple_of(ky * 16 + 8 * z, 8), 8), :] = jnp.where(
                z == 0, modes[:8], modes[8:]
            )
            zout[pl.ds(pl.multiple_of(ky * 8, 8), 8), :] = jnp.where(z == 0, modes[8:], modes[:8])

    pl.semaphore_wait(barrier, PLANE + DP - 1)
    for part in range(4):
        z_copy(part).start()

    pltpu.make_async_remote_copy(
        src_ref=zout3, dst_ref=send4.at[:, 1 - z], send_sem=send_sem.at[3], recv_sem=recv_sem.at[3],
        device_id={"gx": across}, device_id_type=MESH,
    ).wait_recv()

    @pl.loop(0, PLANE - 1)
    def _(step):
        send_copy(far_pair(y, x, step)).start()

    mine = pl.ds(pl.multiple_of(place * 16, 16), 16)
    recv[mine, :] = send[mine, :]

    later[4].wait()
    pw_rows = dot(repeat16, pw[...]).astype(BF)
    kron = dot_nt(pw_rows, repeat16)
    rows_i = lax.broadcasted_iota(jnp.int32, (512, 512), 0)
    cols_i = lax.broadcasted_iota(jnp.int32, (512, 512), 1)
    kron = jnp.where(lax.rem(rows_i, 16) == lax.rem(cols_i, 16), kron, 0.0).astype(BF)
    for g in range(8):
        block = cx[:, 16 * g : 16 * g + 16, :].reshape(512, 128)
        lin[:, 16 * g : 16 * g + 16, :] = dot(kron, block).reshape(32, 16, 128)

    def drain(buffer, rows, index):
        return pltpu.make_async_remote_copy(
            src_ref=buffer[0].at[rows], dst_ref=buffer[1].at[rows],
            send_sem=send_sem.at[index], recv_sem=recv_sem.at[index],
            device_id={"gx": across}, device_id_type=MESH,
        )

    zero = drain((zout, recv), pl.ds(0, 256), 3)
    first = drain((send, recv), pl.ds(0, 496), 0)
    first.wait_recv()

    cols = []
    for q in range(8):
        high, low = split(recv[pl.ds(q, 64, stride=8), :])
        cols.append(jnp.concatenate([high, low], 0))
    modes_x = dot(fwd_x[...], jnp.concatenate(cols, 1))
    modes_x = modes_x[:64] + modes_x[64:]
    modes = []
    for q in range(8):
        part = modes_x[:, 128 * q : 128 * q + 128]
        part = part[:32] + sign * pltpu.roll(part[32:], 64, 1)
        mb[pl.ds(q, 32, stride=8), :] = part
        modes.append(part)

    def dp_copy(target):
        return pltpu.make_async_remote_copy(
            src_ref=mb.at[pl.ds(pl.multiple_of(target * 32, 32), 32)],
            dst_ref=wgr.at[pl.ds(pl.multiple_of(dp * 32, 32), 32)],
            send_sem=send_sem.at[1],
            recv_sem=recv_sem.at[1],
            device_id={"dp": target},
            device_id_type=MESH,
        )

    @pl.loop(1, DP)
    def _(step):
        dp_copy(lax.rem(dp + step, DP)).start()

    ours = pl.ds(pl.multiple_of(dp * 32, 32), 32)
    wgr[ours, :] = mb[ours, :]

    for copy in later[:2]:
        copy.wait()
    high, low = split(jnp.concatenate(modes, 0))
    spread = dot(jnp.concatenate([high, low], 1), spread_cot[...])
    for q in range(8):
        cr = spread[32 * q : 32 * q + 32, :128]
        ci = spread[32 * q : 32 * q + 32, 128:]
        for a in range(4):
            for g in range(2):
                col = 256 * a + 128 * g
                wr = wv[q, :, col : col + 128].astype(F32)
                wi = wv[q, :, 1024 + col : 1024 + col + 128].astype(F32)
                for r, value in enumerate((cr * wr + ci * wi, ci * wr - cr * wi)):
                    high, low = split(value)
                    at = 512 * q + 256 * r + 128 * g
                    prod[32 * a : 32 * a + 32, at : at + 128] = high
                    prod[128 + 32 * a : 160 + 32 * a, at : at + 128] = low
    grad = dot(prod[...], sums[...])
    grad = grad[:128] + grad[128:]
    pieces = [
        jnp.concatenate([grad[32 * a : 32 * a + 32, :128], grad[32 * a : 32 * a + 32, 128:]], 0)
        for a in range(4)
    ]
    high, low = split(jnp.concatenate(pieces, 1))
    back = dot(inv_x[...], jnp.concatenate([high, low, high], 0))
    for a in range(4):
        sb[pl.ds(a, 64, stride=4), :] = back[:, 128 * a : 128 * a + 128]

    sb3 = sb.reshape(64, 4, 128)
    rb3 = rb.reshape(64, 4, 128)

    def back_copy(target):
        return pltpu.make_async_remote_copy(
            src_ref=sb3.at[target],
            dst_ref=rb3.at[me],
            send_sem=send_sem.at[2],
            recv_sem=recv_sem.at[2],
            device_id={"gx": target},
            device_id_type=MESH,
        )

    @pl.loop(0, GX - 1)
    def _(step):
        back_copy(far_first(me, step)).start()

    rb3[me] = sb3[me]

    dp_drain = pltpu.make_async_remote_copy(
        src_ref=mb.at[pl.ds(0, 224)], dst_ref=wgr.at[pl.ds(0, 224)],
        send_sem=send_sem.at[1], recv_sem=recv_sem.at[1],
        device_id={"dp": lax.rem(dp + 1, DP)}, device_id_type=MESH,
    )
    later[3].wait()
    dp_drain.wait_recv()
    high, low = split(wgr[...])
    pair = jnp.concatenate([high, low], 1)
    spread = dot(pair, spread_cot[...])
    cr = spread[:, :128]
    ci = spread[:, 128:]
    for j in range(8):
        inner = dot(pair, spread_in[j])
        ir = inner[:, :128]
        ii = inner[:, 128:]
        for r, value in enumerate((ir * cr + ii * ci, ir * ci - ii * cr)):
            total = value[0:32]
            for s in range(1, 8):
                total = total + value[32 * s : 32 * s + 32]
            at = 1024 * r + 128 * j
            wg_ref[:, :, at : at + 128] = total.reshape(4, 8, 128)

    later[2].wait()
    third = drain((sb, rb), pl.ds(0, 252), 2)
    third.wait_recv()
    tops, bottoms = [], []
    for n in range(8):
        value = rb[pl.ds(n, 32, stride=8), :]
        tops.append(value)
        bottoms.append(jnp.where(odd, pltpu.roll(value, 1, 1), -pltpu.roll(value, 127, 1)))
    stacked = jnp.concatenate([jnp.concatenate(tops, 1), jnp.concatenate(bottoms, 1)], 0)
    high, low = split(stacked)
    along = dot(inv_y[...], jnp.concatenate([high, low, high], 0))
    for a in range(4):
        value = jnp.concatenate(
            [along[:, 128 * a : 128 * a + 128], along[:, 512 + 128 * a : 640 + 128 * a]], 1
        )
        high, low = split(value)
        both = jnp.concatenate([high, low], 0)
        for n in range(4):
            part = dot(both, inv_z[:256, 256 * n : 256 * n + 256])
            total = part[:128] + part[128:] + dot(high, inv_z[256:, 256 * n : 256 * n + 256])
            for u in range(2):
                c = 8 * a + 2 * n + u
                out_ref[0, 0, c] = (total[:, 128 * u : 128 * u + 128] + lin[c]).astype(BF)

    zero.wait_send()
    first.wait_send()
    dp_drain.wait_send()
    third.wait_send()


def on_device(field, cotangent, spectral_weight, pointwise_weight):
    consts = [jnp.asarray(table) for table in tables()]
    operands = [field, cotangent, spectral_weight, pointwise_weight, *consts]
    hbm = pl.BlockSpec(memory_space=pltpu.HBM)
    vmem = pl.BlockSpec(memory_space=pltpu.VMEM)
    field_grad, weight_grad = pl.pallas_call(
        kernel,
        out_shape=(
            jax.ShapeDtypeStruct((1, 1, C, NY, NZ), BF),
            jax.ShapeDtypeStruct((4, 8, 2 * C * C), F32),
        ),
        in_specs=[hbm] * 8,
        out_specs=(vmem, vmem),
        scratch_shapes=[
            pltpu.VMEM((C, NY, NZ), BF),
            pltpu.VMEM((C, NY, NZ), BF),
            pltpu.VMEM((8, KX, 2 * C * C), BF),
            pltpu.VMEM((C, C), BF),
            pltpu.VMEM((640, 256), BF),
            pltpu.VMEM((512, 1024), BF),
            pltpu.VMEM((4096, 256), BF),
            pltpu.VMEM((8, 256, 256), BF),
            pltpu.VMEM((4096, 128), F32),
            pltpu.VMEM((256, 128), F32),
            pltpu.VMEM((512, 128), F32),
            pltpu.VMEM((512, 128), F32),
            pltpu.VMEM((256, 128), F32),
            pltpu.VMEM((256, 128), F32),
            pltpu.VMEM((256, 4096), BF),
            pltpu.VMEM((256, 128), F32),
            pltpu.VMEM((256, 128), F32),
            pltpu.VMEM((C, NY, NZ), F32),
            pltpu.SemaphoreType.DMA((10,)),
            pltpu.SemaphoreType.DMA((4,)),
            pltpu.SemaphoreType.DMA((4,)),
        ],
        compiler_params=pltpu.CompilerParams(
            collective_id=0, has_side_effects=True, vmem_limit_bytes=48 << 20
        ),
        cost_estimate=pl.CostEstimate(flops=10**10, bytes_accessed=10**7, transcendentals=0),
    )(*[pltpu.with_memory_space_constraint(x, pltpu.HBM) for x in operands])
    return field_grad, jnp.transpose(weight_grad, (1, 0, 2))


def solution(mesh):
    placed = (
        P("dp", "gx", None, None, None),
        P("dp", "gx", None, None, None),
        P("gx", None, None),
        P(),
    )
    return jax.shard_map(
        on_device,
        mesh=mesh,
        in_specs=placed,
        out_specs=(P("dp", "gx", None, None, None), P("gx", "dp", None)),
        check_vma=False,
    )
```

```python
import functools
import math

import jax
import jax.numpy as jnp
import ml_dtypes
import numpy as np
from jax import lax
from jax.experimental import pallas as pl
from jax.experimental.pallas import tpu as pltpu
from jax.sharding import PartitionSpec as P

MESH = pl.DeviceIdType.MESH
BF = jnp.bfloat16
F32 = jnp.float32
C = 32
M = 16
NY = NZ = 128
NX = 64
KX = 32
DP = 8
GX = 64
CELLS = NX * NY * NZ


def halves(table):
    high = table.astype(ml_dtypes.bfloat16)
    low = (table - high.astype(np.float64)).astype(ml_dtypes.bfloat16)
    return high, low


def angles(freqs, length):
    product = np.outer(freqs, np.arange(length)) % length
    return product * (2.0 * math.pi / length)


@functools.cache
def tables():
    freq_y = np.r_[0:M, NY - M : NY]
    freq_x = np.r_[0 : KX // 2, NX - KX // 2 : NX]
    freq_z = np.arange(M)
    ay, ax, az = angles(freq_y, NY), angles(freq_x, NX), angles(freq_z, NZ)

    def stack_rows(table):
        high, low = halves(table)
        return np.concatenate(
            [np.concatenate([high, high], 1), np.concatenate([low, np.zeros_like(low)], 1)], 0
        )

    def stack_three(table):
        high, low = halves(table)
        return np.concatenate([high, high, low], 1)

    fwd_y = np.concatenate(halves(np.concatenate([np.cos(ay), -np.sin(ay)])), 0)
    fwd_z = stack_rows(np.concatenate([np.cos(az), np.sin(az)]))
    fwd_x = stack_rows(np.concatenate([np.cos(ax), np.sin(ax)]))
    inv_x = stack_three(np.concatenate([np.cos(ax), np.sin(ax)]).T)
    inv_y = stack_three(np.concatenate([np.cos(ay), np.sin(ay)]).T)

    wave = np.stack([np.cos(az), -np.sin(az)], 1).reshape(2, 8, 2, NZ)
    inv_z = np.zeros((2, 8, 8, 2, 8, NZ))
    for i in range(8):
        inv_z[:, i, :, :, i] = wave
    inv_z = np.concatenate(halves(inv_z.reshape(256, 1024)), 0)

    sums = np.zeros((8, 2, 8, C, 2, 8, 8, 2), np.float32)
    for q in range(8):
        for i in range(8):
            sums[q, 0, i, :, 0, i, q, 0] = 1
            sums[q, 1, i, :, 0, i, q, 1] = 1
            sums[q, 0, i, :, 1, i, q, 1] = 1
            sums[q, 1, i, :, 1, i, q, 0] = -1
    sums = sums.reshape(4096, 256).astype(ml_dtypes.bfloat16)

    spread_cot = np.zeros((2, 2, 2, C, 2, 4, C), np.float32)
    spread_in = np.zeros((8, 2, 2, 2, C, 2, 4, C), np.float32)
    for r in range(2):
        for o in range(C):
            spread_cot[:, r, 1, o, r, :, o] = 1
        for i in range(C):
            spread_in[i // 4, :, r, 0, i, r, i % 4, :] = 1
    spread_cot = spread_cot.reshape(256, 256).astype(ml_dtypes.bfloat16)
    spread_in = spread_in.reshape(8, 256, 256).astype(ml_dtypes.bfloat16)

    def widen(table):
        return np.pad(table, ((0, 0), (0, 256 - table.shape[1])))

    small = np.concatenate(
        [np.concatenate([fwd_y, fwd_x], 1), fwd_z, widen(inv_x), widen(inv_y), spread_cot], 0
    )
    return small, inv_z, sums, spread_in


def split(value):
    high = value.astype(BF)
    return high, (value - high.astype(F32)).astype(BF)


def dot(left, right):
    return jnp.dot(left, right, preferred_element_type=F32)


def dot_nt(left, right):
    return lax.dot_general(left, right, (((1,), (1,)), ((), ())), preferred_element_type=F32)


def far_first(me, step):
    y, x, z = lax.div(me, 8), lax.rem(lax.div(me, 2), 4), lax.rem(me, 2)
    dz = 1 - lax.div(step, 32)
    ky = far_pair(y, x, lax.rem(step, 32))
    return 2 * ky + lax.rem(z + dz, 2)


def far_pair(y, x, step):
    m, j = lax.div(step, 4), lax.rem(step, 4)
    half = lax.div(m + 1, 2)
    dy = jnp.where(lax.rem(m, 2) == 0, 4 + half, 4 - half)
    dx = jnp.where(j == 3, 0, jnp.where(j == 2, 3, 2 - j))
    return lax.rem(y + dy, 8) * 4 + lax.rem(x + dx, 4)


def kernel(
    field_h, cot_h, weight_h, pw_h, small_h, inv_z_h, sums_h, spread_in_h,
    back_ref, lin, wg_ref, inv_z, inv_y_ref,
    fx, cx, wv, pw, small, sums, spread_in,
    planes, send, recv, mb, wgr, prod, sb, rb, wgs,
    load_sem, send_sem, recv_sem,
):
    dp = lax.axis_index("dp")
    me = lax.axis_index("gx")

    loads = []
    for n, (src, dst) in enumerate(((field_h, fx), (cot_h, cx))):
        for h in range(2):
            loads.append(pltpu.make_async_copy(
                src.at[0, 0, pl.ds(16 * h, 16)], dst.at[pl.ds(16 * h, 16)], load_sem.at[2 * n + h]
            ))
    later = [
        pltpu.make_async_copy(src, dst, load_sem.at[4 + n])
        for n, (src, dst) in enumerate(
            ((weight_h, wv), (sums_h, sums), (inv_z_h, inv_z), (spread_in_h, spread_in), (pw_h, pw))
        )
    ]
    table_load = pltpu.make_async_copy(small_h, small, load_sem.at[9])
    for copy in [table_load] + loads:
        copy.start()
    fwd_y = small.at[0:128, 0:128]
    fwd_x = small.at[0:128, 128:256]
    fwd_z = small.at[128:192]
    inv_x = small.at[192:256, 0:192]
    inv_y = small.at[256:384, 0:192]
    spread_cot = small.at[384:640]

    barrier = pltpu.get_barrier_semaphore()

    @pl.loop(0, GX - 1)
    def _(step):
        pl.semaphore_signal(
            barrier, inc=1, device_id={"gx": far_first(me, step)}, device_id_type=MESH
        )

    @pl.loop(1, DP)
    def _(step):
        pl.semaphore_signal(
            barrier, inc=1, device_id={"dp": lax.rem(dp + step, DP)}, device_id_type=MESH
        )

    lane = lax.broadcasted_iota(jnp.int32, (1, 128), 1)
    sign = jnp.where(lane < 64, 1.0, -1.0).astype(F32)
    odd = lax.rem(lane, 2) == 1
    kz = lax.broadcasted_iota(jnp.int32, (M, 128), 0)
    scale = jnp.where(
        lax.rem(lane, 64) < 32, 1.0, jnp.where(kz == 0, 1.0 / CELLS, 2.0 / CELLS)
    ).astype(F32)
    repeat_row = lax.div(lax.broadcasted_iota(jnp.int32, (512, C), 0), 16)
    repeat_col = lax.broadcasted_iota(jnp.int32, (512, C), 1)
    repeat16 = jnp.where(repeat_row == repeat_col, 1.0, 0.0).astype(BF)

    table_load.wait()

    for n, data in enumerate((fx, cx)):
        for h in range(2):
            loads[2 * n + h].wait()

            @pl.loop(0, 2)
            def _(step):
                for u in range(8):
                    c = 16 * h + 8 * step + u
                    along = dot(fwd_y[...], data[c])
                    planes[pl.ds(pl.multiple_of((32 * n + c) * 64, 64), 64), :] = (
                        along[:64] + along[64:]
                    )

    for copy in later:
        copy.start()

    def send_copy(target):
        rows = pl.ds(pl.multiple_of(target * 8, 8), 8)
        return pltpu.make_async_remote_copy(
            src_ref=send.at[rows],
            dst_ref=recv.at[pl.ds(pl.multiple_of(me * 8, 8), 8)],
            send_sem=send_sem.at[0],
            recv_sem=recv_sem.at[0],
            device_id={"gx": target},
            device_id_type=MESH,
        )

    @pl.loop(0, 4)
    def _(step):
        for u in range(8):
            ky = 8 * step + u
            rows = jnp.concatenate(
                [planes[pl.ds(ky, 64, stride=64), :], planes[pl.ds(32 + ky, 64, stride=64), :]], 0
            )
            high, low = split(rows)
            modes = dot_nt(fwd_z[...], jnp.concatenate([high, low], 1))
            modes = modes[:32] + modes[32:]
            modes = (modes[:16] + sign * pltpu.roll(modes[16:], 64, 1)) * scale
            send[pl.ds(pl.multiple_of(ky * 16, 16), 16), :] = modes

    pl.semaphore_wait(barrier, GX - 1 + DP - 1)

    @pl.loop(0, GX - 1)
    def _(step):
        send_copy(far_first(me, step)).start()

    mine = pl.ds(pl.multiple_of(me * 8, 8), 8)
    recv[mine, :] = send[mine, :]

    later[4].wait()
    pw_rows = dot(repeat16, pw[...]).astype(BF)
    kron = dot_nt(pw_rows, repeat16)
    rows_i = lax.broadcasted_iota(jnp.int32, (512, 512), 0)
    cols_i = lax.broadcasted_iota(jnp.int32, (512, 512), 1)
    kron = jnp.where(lax.rem(rows_i, 16) == lax.rem(cols_i, 16), kron, 0.0).astype(BF)
    for g in range(8):
        block = cx[:, 16 * g : 16 * g + 16, :].reshape(512, 128)
        lin[:, 16 * g : 16 * g + 16, :] = dot(kron, block).reshape(32, 16, 128)

    def drain(buffer, rows, index):
        return pltpu.make_async_remote_copy(
            src_ref=buffer[0].at[rows], dst_ref=buffer[1].at[rows],
            send_sem=send_sem.at[index], recv_sem=recv_sem.at[index],
            device_id={"gx": lax.rem(me + 1, GX)}, device_id_type=MESH,
        )

    first = drain((send, recv), pl.ds(0, 504), 0)
    first.wait_recv()

    cols = []
    for q in range(8):
        high, low = split(recv[pl.ds(q, 64, stride=8), :])
        cols.append(jnp.concatenate([high, low], 0))
    modes_x = dot(fwd_x[...], jnp.concatenate(cols, 1))
    modes_x = modes_x[:64] + modes_x[64:]
    modes = []
    for q in range(8):
        part = modes_x[:, 128 * q : 128 * q + 128]
        part = part[:32] + sign * pltpu.roll(part[32:], 64, 1)
        mb[pl.ds(q, 32, stride=8), :] = part
        modes.append(part)

    def dp_copy(target):
        return pltpu.make_async_remote_copy(
            src_ref=mb.at[pl.ds(pl.multiple_of(target * 32, 32), 32)],
            dst_ref=wgr.at[pl.ds(pl.multiple_of(dp * 32, 32), 32)],
            send_sem=send_sem.at[1],
            recv_sem=recv_sem.at[1],
            device_id={"dp": target},
            device_id_type=MESH,
        )

    @pl.loop(1, DP)
    def _(step):
        dp_copy(lax.rem(dp + step, DP)).start()

    ours = pl.ds(pl.multiple_of(dp * 32, 32), 32)
    wgr[ours, :] = mb[ours, :]

    for copy in later[:2]:
        copy.wait()
    high, low = split(jnp.concatenate(modes, 0))
    spread = dot(jnp.concatenate([high, low], 1), spread_cot[...])
    for q in range(8):
        cr = spread[32 * q : 32 * q + 32, :128]
        ci = spread[32 * q : 32 * q + 32, 128:]
        for a in range(4):
            for g in range(2):
                col = 256 * a + 128 * g
                wr = wv[q, :, col : col + 128].astype(F32)
                wi = wv[q, :, 1024 + col : 1024 + col + 128].astype(F32)
                for r, value in enumerate((cr * wr + ci * wi, ci * wr - cr * wi)):
                    high, low = split(value)
                    at = 512 * q + 256 * r + 128 * g
                    prod[32 * a : 32 * a + 32, at : at + 128] = high
                    prod[128 + 32 * a : 160 + 32 * a, at : at + 128] = low
    grad = dot(prod[...], sums[...])
    grad = grad[:128] + grad[128:]
    pieces = [
        jnp.concatenate([grad[32 * a : 32 * a + 32, :128], grad[32 * a : 32 * a + 32, 128:]], 0)
        for a in range(4)
    ]
    high, low = split(jnp.concatenate(pieces, 1))
    back = dot(inv_x[...], jnp.concatenate([high, low, high], 0))
    for a in range(4):
        sb[pl.ds(a, 64, stride=4), :] = back[:, 128 * a : 128 * a + 128]

    sb3 = sb.reshape(64, 4, 128)
    rb3 = rb.reshape(64, 4, 128)

    def back_copy(target):
        return pltpu.make_async_remote_copy(
            src_ref=sb3.at[target],
            dst_ref=rb3.at[me],
            send_sem=send_sem.at[2],
            recv_sem=recv_sem.at[2],
            device_id={"gx": target},
            device_id_type=MESH,
        )

    @pl.loop(0, GX - 1)
    def _(step):
        back_copy(far_first(me, step)).start()

    rb3[me] = sb3[me]

    dp_drain = pltpu.make_async_remote_copy(
        src_ref=mb.at[pl.ds(0, 224)], dst_ref=wgr.at[pl.ds(0, 224)],
        send_sem=send_sem.at[1], recv_sem=recv_sem.at[1],
        device_id={"dp": lax.rem(dp + 1, DP)}, device_id_type=MESH,
    )
    later[3].wait()
    dp_drain.wait_recv()
    high, low = split(wgr[...])
    pair = jnp.concatenate([high, low], 1)
    spread = dot(pair, spread_cot[...])
    cr = spread[:, :128]
    ci = spread[:, 128:]
    for j in range(8):
        inner = dot(pair, spread_in[j])
        ir = inner[:, :128]
        ii = inner[:, 128:]
        for r, value in enumerate((ir * cr + ii * ci, ir * ci - ii * cr)):
            total = value[0:32]
            for s in range(1, 8):
                total = total + value[32 * s : 32 * s + 32]
            at = 1024 * r + 128 * j
            wgs[at // 4 : at // 4 + 32, :] = total
    for q in range(8):
        for n in range(16):
            wg_ref[q, :, 128 * n : 128 * n + 128] = wgs[pl.ds(32 * n + q, 4, stride=8), :]

    inv_y_ref[...] = small[256:384, 0:192]
    later[2].wait()
    third = drain((sb, rb), pl.ds(0, 252), 2)
    third.wait_recv()
    back_ref[...] = rb[...]

    first.wait_send()
    dp_drain.wait_send()
    third.wait_send()


def finish_kernel(back_ref, lin, wg_ref, inv_z, inv_y, out_h, wg_h, out, sem):
    weights = pltpu.make_async_copy(wg_ref, wg_h, sem.at[4])
    weights.start()
    odd = lax.rem(lax.broadcasted_iota(jnp.int32, (1, 128), 1), 2) == 1
    tops, bottoms = [], []
    for n in range(8):
        value = back_ref[pl.ds(n, 32, stride=8), :]
        tops.append(value)
        bottoms.append(jnp.where(odd, pltpu.roll(value, 1, 1), -pltpu.roll(value, 127, 1)))
    stacked = jnp.concatenate([jnp.concatenate(tops, 1), jnp.concatenate(bottoms, 1)], 0)
    high, low = split(stacked)
    along = dot(inv_y[...], jnp.concatenate([high, low, high], 0))
    stores = []
    for a in range(4):
        value = jnp.concatenate(
            [along[:, 128 * a : 128 * a + 128], along[:, 512 + 128 * a : 640 + 128 * a]], 1
        )
        high, low = split(value)
        both = jnp.concatenate([high, low], 0)
        for n in range(4):
            part = dot(both, inv_z[:256, 256 * n : 256 * n + 256])
            total = part[:128] + part[128:] + dot(high, inv_z[256:, 256 * n : 256 * n + 256])
            for u in range(2):
                c = 8 * a + 2 * n + u
                out[c] = (total[:, 128 * u : 128 * u + 128] + lin[c]).astype(BF)
        rows = pl.ds(8 * a, 8)
        stores.append(pltpu.make_async_copy(out.at[rows], out_h.at[0, 0, rows], sem.at[a]))
        stores[-1].start()
    for copy in stores + [weights]:
        copy.wait()


def on_device(field, cotangent, spectral_weight, pointwise_weight):
    consts = [jnp.asarray(table) for table in tables()]
    operands = [field, cotangent, spectral_weight, pointwise_weight, *consts]
    hbm = pl.BlockSpec(memory_space=pltpu.HBM)
    vmem = pl.BlockSpec(memory_space=pltpu.VMEM)
    middle = pl.pallas_call(
        kernel,
        out_shape=(
            jax.ShapeDtypeStruct((256, 128), F32),
            jax.ShapeDtypeStruct((C, NY, NZ), F32),
            jax.ShapeDtypeStruct((8, 4, 2 * C * C), F32),
            jax.ShapeDtypeStruct((512, 1024), BF),
            jax.ShapeDtypeStruct((128, 192), BF),
        ),
        in_specs=[hbm] * 8,
        out_specs=(vmem,) * 5,
        scratch_shapes=[
            pltpu.VMEM((C, NY, NZ), BF),
            pltpu.VMEM((C, NY, NZ), BF),
            pltpu.VMEM((8, KX, 2 * C * C), BF),
            pltpu.VMEM((C, C), BF),
            pltpu.VMEM((640, 256), BF),
            pltpu.VMEM((4096, 256), BF),
            pltpu.VMEM((8, 256, 256), BF),
            pltpu.VMEM((4096, 128), F32),
            pltpu.VMEM((512, 128), F32),
            pltpu.VMEM((512, 128), F32),
            pltpu.VMEM((256, 128), F32),
            pltpu.VMEM((256, 128), F32),
            pltpu.VMEM((256, 4096), BF),
            pltpu.VMEM((256, 128), F32),
            pltpu.VMEM((256, 128), F32),
            pltpu.VMEM((512, 128), F32),
            pltpu.SemaphoreType.DMA((10,)),
            pltpu.SemaphoreType.DMA((3,)),
            pltpu.SemaphoreType.DMA((3,)),
        ],
        compiler_params=pltpu.CompilerParams(
            collective_id=0, has_side_effects=True, vmem_limit_bytes=40 << 20
        ),
        cost_estimate=pl.CostEstimate(flops=10**10, bytes_accessed=10**7, transcendentals=0),
    )(*[pltpu.with_memory_space_constraint(x, pltpu.HBM) for x in operands])
    return pl.pallas_call(
        finish_kernel,
        out_shape=(
            jax.ShapeDtypeStruct((1, 1, C, NY, NZ), BF),
            jax.ShapeDtypeStruct((8, 4, 2 * C * C), F32),
        ),
        in_specs=[vmem] * 5,
        out_specs=(hbm, hbm),
        scratch_shapes=[pltpu.VMEM((C, NY, NZ), BF), pltpu.SemaphoreType.DMA((5,))],
        compiler_params=pltpu.CompilerParams(vmem_limit_bytes=12 << 20),
        cost_estimate=pl.CostEstimate(flops=10**9, bytes_accessed=10**6, transcendentals=0),
    )(*middle)


def solution(mesh):
    placed = (
        P("dp", "gx", None, None, None),
        P("dp", "gx", None, None, None),
        P("gx", None, None),
        P(),
    )
    return jax.shard_map(
        on_device,
        mesh=mesh,
        in_specs=placed,
        out_specs=(P("dp", "gx", None, None, None), P("gx", "dp", None)),
        check_vma=False,
    )
```

```python
import functools
import math

import jax
import jax.numpy as jnp
import ml_dtypes
import numpy as np
from jax import lax
from jax.experimental import pallas as pl
from jax.experimental.pallas import tpu as pltpu
from jax.sharding import PartitionSpec as P

MESH = pl.DeviceIdType.MESH
BF = jnp.bfloat16
F32 = jnp.float32
C = 32
M = 16
NY = NZ = 128
NX = 64
KX = 32
DP = 8
GX = 64
CELLS = NX * NY * NZ


def halves(table):
    high = table.astype(ml_dtypes.bfloat16)
    low = (table - high.astype(np.float64)).astype(ml_dtypes.bfloat16)
    return high, low


def angles(freqs, length):
    product = np.outer(freqs, np.arange(length)) % length
    return product * (2.0 * math.pi / length)


@functools.cache
def tables():
    freq_y = np.r_[0:M, NY - M : NY]
    freq_x = np.r_[0 : KX // 2, NX - KX // 2 : NX]
    freq_z = np.arange(M)
    ay, ax, az = angles(freq_y, NY), angles(freq_x, NX), angles(freq_z, NZ)

    def stack_rows(table):
        high, low = halves(table)
        return np.concatenate(
            [np.concatenate([high, high], 1), np.concatenate([low, np.zeros_like(low)], 1)], 0
        )

    def stack_three(table):
        high, low = halves(table)
        return np.concatenate([high, high, low], 1)

    fwd_y = np.concatenate(halves(np.concatenate([np.cos(ay), -np.sin(ay)])), 0)
    fwd_z = stack_rows(np.concatenate([np.cos(az), np.sin(az)]))
    fwd_x = stack_rows(np.concatenate([np.cos(ax), np.sin(ax)]))
    inv_x = np.zeros((4, NX, 2, 4, KX))
    for a in range(4):
        inv_x[a, :, 0, a] = np.cos(ax).T
        inv_x[a, :, 1, a] = np.sin(ax).T
    inv_x = np.concatenate(halves(inv_x.reshape(256, 256)), 0)
    inv_y = stack_three(np.concatenate([np.cos(ay), np.sin(ay)]).T)

    wave = np.stack([np.cos(az), -np.sin(az)], 1).reshape(2, 8, 2, NZ)
    inv_z = np.zeros((2, 8, 2, 8, 8, NZ))
    for i in range(8):
        inv_z[:, :, :, i, i] = wave
    inv_z = np.concatenate(halves(inv_z.reshape(256, 1024)), 0)

    sums = np.repeat(np.eye(8), C, 1).astype(ml_dtypes.bfloat16)

    spread_cot = np.zeros((2, 2, 2, C, 2, 4, C), np.float32)
    spread_in = np.zeros((8, 2, 2, 2, C, 2, 4, C), np.float32)
    for r in range(2):
        for o in range(C):
            spread_cot[:, r, 1, o, r, :, o] = 1
        for i in range(C):
            spread_in[i // 4, :, r, 0, i, r, i % 4, :] = 1
    spread_cot = spread_cot.reshape(256, 256).astype(ml_dtypes.bfloat16)
    spread_in = spread_in.reshape(8, 256, 256).astype(ml_dtypes.bfloat16)

    def widen(table):
        return np.pad(table, ((0, 0), (0, 256 - table.shape[1])))

    small = np.concatenate(
        [np.concatenate([fwd_y, fwd_x], 1), fwd_z, widen(inv_y), spread_cot, inv_x, sums], 0
    )
    return small, inv_z, spread_in


def split(value):
    high = value.astype(BF)
    return high, (value - high.astype(F32)).astype(BF)


def dot(left, right):
    return jnp.dot(left, right, preferred_element_type=F32)


def dot_nt(left, right):
    return lax.dot_general(left, right, (((1,), (1,)), ((), ())), preferred_element_type=F32)


def far_first(me, step):
    y, x, z = lax.div(me, 8), lax.rem(lax.div(me, 2), 4), lax.rem(me, 2)
    dz = 1 - lax.div(step, 32)
    ky = far_pair(y, x, lax.rem(step, 32))
    return 2 * ky + lax.rem(z + dz, 2)


def far_pair(y, x, step):
    m, j = lax.div(step, 4), lax.rem(step, 4)
    half = lax.div(m + 1, 2)
    dy = jnp.where(lax.rem(m, 2) == 0, 4 + half, 4 - half)
    dx = jnp.where(j == 3, 0, jnp.where(j == 2, 3, 2 - j))
    return lax.rem(y + dy, 8) * 4 + lax.rem(x + dx, 4)


def kernel(
    field_h, cot_h, weight_h, pw_h, small_h, inv_z_h, spread_in_h,
    back_ref, lin, wg_ref, inv_z, inv_y_ref,
    fx, cx, wv, pw, small, spread_in,
    planes, send, recv, mb, wgr, prod, sb, rb, wgs,
    load_sem, send_sem, recv_sem,
):
    dp = lax.axis_index("dp")
    me = lax.axis_index("gx")

    loads = []
    for n, (src, dst) in enumerate(((field_h, fx), (cot_h, cx))):
        for h in range(2):
            loads.append(pltpu.make_async_copy(
                src.at[0, 0, pl.ds(16 * h, 16)], dst.at[pl.ds(16 * h, 16)], load_sem.at[2 * n + h]
            ))
    later = [
        pltpu.make_async_copy(src, dst, load_sem.at[4 + n])
        for n, (src, dst) in enumerate(
            ((weight_h, wv), (inv_z_h, inv_z), (spread_in_h, spread_in), (pw_h, pw))
        )
    ]
    table_load = pltpu.make_async_copy(small_h, small, load_sem.at[8])
    for copy in [table_load] + loads:
        copy.start()
    fwd_y = small.at[0:128, 0:128]
    fwd_x = small.at[0:128, 128:256]
    fwd_z = small.at[128:192]
    spread_cot = small.at[320:576]
    inv_x = small.at[576:1088]
    sums = small.at[1088:1096]

    barrier = pltpu.get_barrier_semaphore()

    @pl.loop(0, GX - 1)
    def _(step):
        pl.semaphore_signal(
            barrier, inc=1, device_id={"gx": far_first(me, step)}, device_id_type=MESH
        )

    @pl.loop(1, DP)
    def _(step):
        pl.semaphore_signal(
            barrier, inc=1, device_id={"dp": lax.rem(dp + step, DP)}, device_id_type=MESH
        )

    lane = lax.broadcasted_iota(jnp.int32, (1, 128), 1)
    sign = jnp.where(lane < 64, 1.0, -1.0).astype(F32)
    kz = lax.broadcasted_iota(jnp.int32, (M, 128), 0)
    scale = jnp.where(
        lax.rem(lane, 64) < 32, 1.0, jnp.where(kz == 0, 1.0 / CELLS, 2.0 / CELLS)
    ).astype(F32)
    repeat_row = lax.div(lax.broadcasted_iota(jnp.int32, (512, C), 0), 16)
    repeat_col = lax.broadcasted_iota(jnp.int32, (512, C), 1)
    repeat16 = jnp.where(repeat_row == repeat_col, 1.0, 0.0).astype(BF)

    table_load.wait()

    for n, data in enumerate((fx, cx)):
        for h in range(2):
            loads[2 * n + h].wait()

            @pl.loop(0, 2)
            def _(step):
                for u in range(8):
                    c = 16 * h + 8 * step + u
                    along = dot(fwd_y[...], data[c])
                    planes[pl.ds(pl.multiple_of((32 * n + c) * 64, 64), 64), :] = (
                        along[:64] + along[64:]
                    )

    for copy in later:
        copy.start()

    def send_copy(target):
        rows = pl.ds(pl.multiple_of(target * 8, 8), 8)
        return pltpu.make_async_remote_copy(
            src_ref=send.at[rows],
            dst_ref=recv.at[pl.ds(pl.multiple_of(me * 8, 8), 8)],
            send_sem=send_sem.at[0],
            recv_sem=recv_sem.at[0],
            device_id={"gx": target},
            device_id_type=MESH,
        )

    @pl.loop(0, 4)
    def _(step):
        for u in range(8):
            ky = 8 * step + u
            rows = jnp.concatenate(
                [planes[pl.ds(ky, 64, stride=64), :], planes[pl.ds(32 + ky, 64, stride=64), :]], 0
            )
            high, low = split(rows)
            modes = dot_nt(fwd_z[...], jnp.concatenate([high, low], 1))
            modes = modes[:32] + modes[32:]
            modes = (modes[:16] + sign * pltpu.roll(modes[16:], 64, 1)) * scale
            send[pl.ds(pl.multiple_of(ky * 16, 16), 16), :] = modes

    pl.semaphore_wait(barrier, GX - 1 + DP - 1)

    @pl.loop(0, GX - 1)
    def _(step):
        send_copy(far_first(me, step)).start()

    mine = pl.ds(pl.multiple_of(me * 8, 8), 8)
    recv[mine, :] = send[mine, :]

    later[3].wait()
    pw_rows = dot(repeat16, pw[...]).astype(BF)
    kron = dot_nt(pw_rows, repeat16)
    rows_i = lax.broadcasted_iota(jnp.int32, (512, 512), 0)
    cols_i = lax.broadcasted_iota(jnp.int32, (512, 512), 1)
    kron = jnp.where(lax.rem(rows_i, 16) == lax.rem(cols_i, 16), kron, 0.0).astype(BF)
    for g in range(8):
        block = cx[:, 16 * g : 16 * g + 16, :].reshape(512, 128)
        lin[:, 16 * g : 16 * g + 16, :] = dot(kron, block).reshape(32, 16, 128)

    def drain(buffer, rows, index):
        return pltpu.make_async_remote_copy(
            src_ref=buffer[0].at[rows], dst_ref=buffer[1].at[rows],
            send_sem=send_sem.at[index], recv_sem=recv_sem.at[index],
            device_id={"gx": lax.rem(me + 1, GX)}, device_id_type=MESH,
        )

    first = drain((send, recv), pl.ds(0, 504), 0)
    first.wait_recv()

    cols = []
    for q in range(8):
        high, low = split(recv[pl.ds(q, 64, stride=8), :])
        cols.append(jnp.concatenate([high, low], 0))
    modes_x = dot(fwd_x[...], jnp.concatenate(cols, 1))
    modes_x = modes_x[:64] + modes_x[64:]
    modes = []
    for q in range(8):
        part = modes_x[:, 128 * q : 128 * q + 128]
        part = part[:32] + sign * pltpu.roll(part[32:], 64, 1)
        mb[pl.ds(q, 32, stride=8), :] = part
        modes.append(part)

    def dp_copy(target):
        return pltpu.make_async_remote_copy(
            src_ref=mb.at[pl.ds(pl.multiple_of(target * 32, 32), 32)],
            dst_ref=wgr.at[pl.ds(pl.multiple_of(dp * 32, 32), 32)],
            send_sem=send_sem.at[1],
            recv_sem=recv_sem.at[1],
            device_id={"dp": target},
            device_id_type=MESH,
        )

    @pl.loop(1, DP)
    def _(step):
        dp_copy(lax.rem(dp + step, DP)).start()

    ours = pl.ds(pl.multiple_of(dp * 32, 32), 32)
    wgr[ours, :] = mb[ours, :]

    later[0].wait()
    high, low = split(jnp.concatenate(modes, 0))
    spread = dot(jnp.concatenate([high, low], 1), spread_cot[...])
    for q in range(8):
        cr = spread[32 * q : 32 * q + 32, :128]
        ci = spread[32 * q : 32 * q + 32, 128:]
        for a in range(4):
            for g in range(2):
                col = 256 * a + 128 * g
                wr = wv[q, :, col : col + 128].astype(F32)
                wi = wv[q, :, 1024 + col : 1024 + col + 128].astype(F32)
                for r, value in enumerate((cr * wr + ci * wi, ci * wr - cr * wi)):
                    high, low = split(value)
                    cols = slice(128 * g, 128 * g + 128)
                    prod[2 * q + r, 32 * a : 32 * a + 32, cols] = high
                    prod[2 * q + r, 128 + 32 * a : 160 + 32 * a, cols] = low
    plain, turned = [], []
    for q in range(8):
        re, im = [dot_nt(sums[...], prod[2 * q + r]) for r in range(2)]
        re = re[:, :128] + re[:, 128:]
        im = im[:, :128] + im[:, 128:]
        plain += [re, im]
        turned += [-im, re]
    grad = jnp.concatenate([jnp.concatenate(plain, 0), jnp.concatenate(turned, 0)], 1)
    high, low = split(grad)
    back = dot_nt(inv_x[...], high)
    back = back[:256] + back[256:] + dot_nt(inv_x[:256], low)
    for a in range(4):
        sb[pl.ds(a, 64, stride=4), :] = back[64 * a : 64 * a + 64]

    sb3 = sb.reshape(64, 4, 128)
    rb3 = rb.reshape(64, 4, 128)

    def back_copy(target):
        return pltpu.make_async_remote_copy(
            src_ref=sb3.at[target],
            dst_ref=rb3.at[me],
            send_sem=send_sem.at[2],
            recv_sem=recv_sem.at[2],
            device_id={"gx": target},
            device_id_type=MESH,
        )

    @pl.loop(0, GX - 1)
    def _(step):
        back_copy(far_first(me, step)).start()

    rb3[me] = sb3[me]

    dp_drain = pltpu.make_async_remote_copy(
        src_ref=mb.at[pl.ds(0, 224)], dst_ref=wgr.at[pl.ds(0, 224)],
        send_sem=send_sem.at[1], recv_sem=recv_sem.at[1],
        device_id={"dp": lax.rem(dp + 1, DP)}, device_id_type=MESH,
    )
    later[2].wait()
    dp_drain.wait_recv()
    high, low = split(wgr[...])
    pair = jnp.concatenate([high, low], 1)
    spread = dot(pair, spread_cot[...])
    cr = spread[:, :128]
    ci = spread[:, 128:]
    for j in range(8):
        inner = dot(pair, spread_in[j])
        ir = inner[:, :128]
        ii = inner[:, 128:]
        for r, value in enumerate((ir * cr + ii * ci, ir * ci - ii * cr)):
            total = value[0:32]
            for s in range(1, 8):
                total = total + value[32 * s : 32 * s + 32]
            at = 1024 * r + 128 * j
            wgs[at // 4 : at // 4 + 32, :] = total
    for q in range(8):
        for n in range(16):
            wg_ref[q, :, 128 * n : 128 * n + 128] = wgs[pl.ds(32 * n + q, 4, stride=8), :]

    inv_y_ref[...] = small[192:320, 0:192]
    later[1].wait()
    third = drain((sb, rb), pl.ds(0, 252), 2)
    third.wait_recv()
    back_ref[...] = rb[...]

    first.wait_send()
    dp_drain.wait_send()
    third.wait_send()


def finish_kernel(back_ref, lin, wg_ref, inv_z, inv_y, out_h, wg_h, out, sem):
    weights = pltpu.make_async_copy(wg_ref, wg_h, sem.at[4])
    weights.start()
    imag = (lax.broadcasted_iota(jnp.int32, (1, 128), 1) & 8) != 0
    tops, bottoms = [], []
    for n in range(8):
        value = back_ref[pl.ds(n, 32, stride=8), :]
        tops.append(value)
        bottoms.append(jnp.where(imag, pltpu.roll(value, 8, 1), -pltpu.roll(value, 120, 1)))
    stacked = jnp.concatenate([jnp.concatenate(tops, 1), jnp.concatenate(bottoms, 1)], 0)
    high, low = split(stacked)
    along = dot(inv_y[...], jnp.concatenate([high, low, high], 0))
    stores = []
    for a in range(4):
        value = jnp.concatenate(
            [along[:, 128 * a : 128 * a + 128], along[:, 512 + 128 * a : 640 + 128 * a]], 1
        )
        high, low = split(value)
        both = jnp.concatenate([high, low], 0)
        for n in range(4):
            part = dot(both, inv_z[:256, 256 * n : 256 * n + 256])
            total = part[:128] + part[128:] + dot(high, inv_z[256:, 256 * n : 256 * n + 256])
            for u in range(2):
                c = 8 * a + 2 * n + u
                out[c] = (total[:, 128 * u : 128 * u + 128] + lin[c]).astype(BF)
        rows = pl.ds(8 * a, 8)
        stores.append(pltpu.make_async_copy(out.at[rows], out_h.at[0, 0, rows], sem.at[a]))
        stores[-1].start()
    for copy in stores + [weights]:
        copy.wait()


def on_device(field, cotangent, spectral_weight, pointwise_weight):
    consts = [jnp.asarray(table) for table in tables()]
    operands = [field, cotangent, spectral_weight, pointwise_weight, *consts]
    hbm = pl.BlockSpec(memory_space=pltpu.HBM)
    vmem = pl.BlockSpec(memory_space=pltpu.VMEM)
    middle = pl.pallas_call(
        kernel,
        out_shape=(
            jax.ShapeDtypeStruct((256, 128), F32),
            jax.ShapeDtypeStruct((C, NY, NZ), F32),
            jax.ShapeDtypeStruct((8, 4, 2 * C * C), F32),
            jax.ShapeDtypeStruct((512, 1024), BF),
            jax.ShapeDtypeStruct((128, 192), BF),
        ),
        in_specs=[hbm] * 7,
        out_specs=(vmem,) * 5,
        scratch_shapes=[
            pltpu.VMEM((C, NY, NZ), BF),
            pltpu.VMEM((C, NY, NZ), BF),
            pltpu.VMEM((8, KX, 2 * C * C), BF),
            pltpu.VMEM((C, C), BF),
            pltpu.VMEM((1096, 256), BF),
            pltpu.VMEM((8, 256, 256), BF),
            pltpu.VMEM((4096, 128), F32),
            pltpu.VMEM((512, 128), F32),
            pltpu.VMEM((512, 128), F32),
            pltpu.VMEM((256, 128), F32),
            pltpu.VMEM((256, 128), F32),
            pltpu.VMEM((16, 256, 256), BF),
            pltpu.VMEM((256, 128), F32),
            pltpu.VMEM((256, 128), F32),
            pltpu.VMEM((512, 128), F32),
            pltpu.SemaphoreType.DMA((9,)),
            pltpu.SemaphoreType.DMA((3,)),
            pltpu.SemaphoreType.DMA((3,)),
        ],
        compiler_params=pltpu.CompilerParams(
            collective_id=0, has_side_effects=True, vmem_limit_bytes=40 << 20
        ),
        cost_estimate=pl.CostEstimate(flops=10**10, bytes_accessed=10**7, transcendentals=0),
    )(*[pltpu.with_memory_space_constraint(x, pltpu.HBM) for x in operands])
    return pl.pallas_call(
        finish_kernel,
        out_shape=(
            jax.ShapeDtypeStruct((1, 1, C, NY, NZ), BF),
            jax.ShapeDtypeStruct((8, 4, 2 * C * C), F32),
        ),
        in_specs=[vmem] * 5,
        out_specs=(hbm, hbm),
        scratch_shapes=[pltpu.VMEM((C, NY, NZ), BF), pltpu.SemaphoreType.DMA((5,))],
        compiler_params=pltpu.CompilerParams(vmem_limit_bytes=12 << 20),
        cost_estimate=pl.CostEstimate(flops=10**9, bytes_accessed=10**6, transcendentals=0),
    )(*middle)


def solution(mesh):
    placed = (
        P("dp", "gx", None, None, None),
        P("dp", "gx", None, None, None),
        P("gx", None, None),
        P(),
    )
    return jax.shard_map(
        on_device,
        mesh=mesh,
        in_specs=placed,
        out_specs=(P("dp", "gx", None, None, None), P("gx", "dp", None)),
        check_vma=False,
    )
```

```python
import functools
import math

import jax
import jax.numpy as jnp
import ml_dtypes
import numpy as np
from jax import lax
from jax.experimental import pallas as pl
from jax.experimental.pallas import tpu as pltpu
from jax.sharding import PartitionSpec as P

MESH = pl.DeviceIdType.MESH
BF = jnp.bfloat16
F32 = jnp.float32
C = 32
M = 16
NY = NZ = 128
NX = 64
KX = 32
DP = 8
GX = 64
CELLS = NX * NY * NZ


def halves(table):
    high = table.astype(ml_dtypes.bfloat16)
    low = (table - high.astype(np.float64)).astype(ml_dtypes.bfloat16)
    return high, low


def angles(freqs, length):
    product = np.outer(freqs, np.arange(length)) % length
    return product * (2.0 * math.pi / length)


@functools.cache
def tables():
    freq_y = np.r_[0:M, NY - M : NY]
    freq_x = np.r_[0 : KX // 2, NX - KX // 2 : NX]
    freq_z = np.arange(M)
    ay, ax, az = angles(freq_y, NY), angles(freq_x, NX), angles(freq_z, NZ)

    def stack_rows(table):
        high, low = halves(table)
        return np.concatenate(
            [np.concatenate([high, high], 1), np.concatenate([low, np.zeros_like(low)], 1)], 0
        )

    def stack_three(table):
        high, low = halves(table)
        return np.concatenate([high, high, low], 1)

    fwd_y = np.concatenate(halves(np.concatenate([np.cos(ay), -np.sin(ay)])), 0)
    fwd_z = stack_rows(np.concatenate([np.cos(az), np.sin(az)]))
    fwd_x = stack_rows(np.concatenate([np.cos(ax), np.sin(ax)]))
    inv_x = np.zeros((4, NX, 2, 4, KX))
    for a in range(4):
        inv_x[a, :, 0, a] = np.cos(ax).T
        inv_x[a, :, 1, a] = np.sin(ax).T
    inv_x = np.concatenate(halves(inv_x.reshape(256, 256)), 0)
    inv_y = stack_three(np.concatenate([np.cos(ay), np.sin(ay)]).T)

    wave = np.stack([np.cos(az), -np.sin(az)], 1).reshape(2, 8, 2, NZ)
    inv_z = np.zeros((2, 8, 2, 8, 8, NZ))
    for i in range(8):
        inv_z[:, :, :, i, i] = wave
    inv_z = np.concatenate(halves(inv_z.reshape(256, 1024)), 0)

    sums = np.repeat(np.eye(8), C, 1).astype(ml_dtypes.bfloat16)

    spread_cot = np.zeros((2, 2, 2, C, 2, 4, C), np.float32)
    spread_in = np.zeros((8, 2, 2, 2, C, 2, 4, C), np.float32)
    for r in range(2):
        for o in range(C):
            spread_cot[:, r, 1, o, r, :, o] = 1
        for i in range(C):
            spread_in[i // 4, :, r, 0, i, r, i % 4, :] = 1
    spread_cot = spread_cot.reshape(256, 256).astype(ml_dtypes.bfloat16)
    spread_in = spread_in.reshape(8, 256, 256).astype(ml_dtypes.bfloat16)

    def widen(table):
        return np.pad(table, ((0, 0), (0, 256 - table.shape[1])))

    small = np.concatenate(
        [np.concatenate([fwd_y, fwd_x], 1), fwd_z, widen(inv_y), spread_cot, inv_x, sums], 0
    )
    return small, inv_z, spread_in


def split(value):
    high = value.astype(BF)
    return high, (value - high.astype(F32)).astype(BF)


def dot(left, right):
    return jnp.dot(left, right, preferred_element_type=F32)


def dot_nt(left, right):
    return lax.dot_general(left, right, (((1,), (1,)), ((), ())), preferred_element_type=F32)


def far_first(me, step):
    y, x, z = lax.div(me, 8), lax.rem(lax.div(me, 2), 4), lax.rem(me, 2)
    dz = 1 - lax.div(step, 32)
    ky = far_pair(y, x, lax.rem(step, 32))
    return 2 * ky + lax.rem(z + dz, 2)


def far_pair(y, x, step):
    m, j = lax.div(step, 4), lax.rem(step, 4)
    half = lax.div(m + 1, 2)
    dy = jnp.where(lax.rem(m, 2) == 0, 4 + half, 4 - half)
    dx = jnp.where(j == 3, 0, jnp.where(j == 2, 3, 2 - j))
    return lax.rem(y + dy, 8) * 4 + lax.rem(x + dx, 4)


def kernel(
    field_h, cot_h, weight_h, pw_h, small_h, inv_z_h, spread_in_h,
    back_ref, lin, wg_ref, inv_z, inv_y_ref,
    fx, cx, wv, pw, small, spread_in,
    planes, send, recv, mb, wgr, prod, sb, rb, wgs,
    load_sem, send_sem, recv_sem,
):
    dp = lax.axis_index("dp")
    me = lax.axis_index("gx")

    barrier = pltpu.get_barrier_semaphore()

    @pl.loop(0, GX // 2)
    def _(step):
        pl.semaphore_signal(
            barrier, inc=1, device_id={"gx": far_first(me, step)}, device_id_type=MESH
        )

    loads = []
    for n, (src, dst) in enumerate(((field_h, fx), (cot_h, cx))):
        for h in range(2):
            loads.append(pltpu.make_async_copy(
                src.at[0, 0, pl.ds(16 * h, 16)], dst.at[pl.ds(16 * h, 16)], load_sem.at[2 * n + h]
            ))
    later = [
        pltpu.make_async_copy(src, dst, load_sem.at[4 + n])
        for n, (src, dst) in enumerate(
            ((weight_h, wv), (inv_z_h, inv_z), (spread_in_h, spread_in), (pw_h, pw))
        )
    ]
    table_load = pltpu.make_async_copy(small_h, small, load_sem.at[8])
    for copy in [table_load] + loads:
        copy.start()
    fwd_y = small.at[0:128, 0:128]
    fwd_x = small.at[0:128, 128:256]
    fwd_z = small.at[128:192]
    spread_cot = small.at[320:576]
    inv_x = small.at[576:1088]
    sums = small.at[1088:1096]

    @pl.loop(GX // 2, GX - 1)
    def _(step):
        pl.semaphore_signal(
            barrier, inc=1, device_id={"gx": far_first(me, step)}, device_id_type=MESH
        )

    @pl.loop(1, DP)
    def _(step):
        pl.semaphore_signal(
            barrier, inc=1, device_id={"dp": lax.rem(dp + step, DP)}, device_id_type=MESH
        )

    lane = lax.broadcasted_iota(jnp.int32, (1, 128), 1)
    sign = jnp.where(lane < 64, 1.0, -1.0).astype(F32)
    kz = lax.broadcasted_iota(jnp.int32, (M, 128), 0)
    scale = jnp.where(
        lax.rem(lane, 64) < 32, 1.0, jnp.where(kz == 0, 1.0 / CELLS, 2.0 / CELLS)
    ).astype(F32)
    repeat_row = lax.div(lax.broadcasted_iota(jnp.int32, (512, C), 0), 16)
    repeat_col = lax.broadcasted_iota(jnp.int32, (512, C), 1)
    repeat16 = jnp.where(repeat_row == repeat_col, 1.0, 0.0).astype(BF)

    table_load.wait()

    for n, data in enumerate((fx, cx)):
        for h in range(2):
            loads[2 * n + h].wait()

            @pl.loop(0, 2)
            def _(step):
                for u in range(8):
                    c = 16 * h + 8 * step + u
                    along = dot(fwd_y[...], data[c])
                    planes[pl.ds(pl.multiple_of((32 * n + c) * 64, 64), 64), :] = (
                        along[:64] + along[64:]
                    )

    for copy in later:
        copy.start()

    def send_copy(target):
        rows = pl.ds(pl.multiple_of(target * 8, 8), 8)
        return pltpu.make_async_remote_copy(
            src_ref=send.at[rows],
            dst_ref=recv.at[pl.ds(pl.multiple_of(me * 8, 8), 8)],
            send_sem=send_sem.at[0],
            recv_sem=recv_sem.at[0],
            device_id={"gx": target},
            device_id_type=MESH,
        )

    @pl.loop(0, 4)
    def _(step):
        for u in range(8):
            ky = 8 * step + u
            rows = jnp.concatenate(
                [planes[pl.ds(ky, 64, stride=64), :], planes[pl.ds(32 + ky, 64, stride=64), :]], 0
            )
            high, low = split(rows)
            modes = dot_nt(fwd_z[...], jnp.concatenate([high, low], 1))
            modes = modes[:32] + modes[32:]
            modes = (modes[:16] + sign * pltpu.roll(modes[16:], 64, 1)) * scale
            send[pl.ds(pl.multiple_of(ky * 16, 16), 16), :] = modes

    pl.semaphore_wait(barrier, GX - 1 + DP - 1)

    @pl.loop(0, GX - 1, unroll=9)
    def _(step):
        send_copy(far_first(me, step)).start()

    mine = pl.ds(pl.multiple_of(me * 8, 8), 8)
    recv[mine, :] = send[mine, :]

    later[3].wait()
    pw_rows = dot(repeat16, pw[...]).astype(BF)
    kron = dot_nt(pw_rows, repeat16)
    rows_i = lax.broadcasted_iota(jnp.int32, (512, 512), 0)
    cols_i = lax.broadcasted_iota(jnp.int32, (512, 512), 1)
    kron = jnp.where(lax.rem(rows_i, 16) == lax.rem(cols_i, 16), kron, 0.0).astype(BF)
    for g in range(8):
        block = cx[:, 16 * g : 16 * g + 16, :].reshape(512, 128)
        lin[:, 16 * g : 16 * g + 16, :] = dot(kron, block).reshape(32, 16, 128)

    def drain(buffer, rows, index):
        return pltpu.make_async_remote_copy(
            src_ref=buffer[0].at[rows], dst_ref=buffer[1].at[rows],
            send_sem=send_sem.at[index], recv_sem=recv_sem.at[index],
            device_id={"gx": lax.rem(me + 1, GX)}, device_id_type=MESH,
        )

    first = drain((send, recv), pl.ds(0, 504), 0)
    first.wait_recv()

    cols = []
    for q in range(8):
        high, low = split(recv[pl.ds(q, 64, stride=8), :])
        cols.append(jnp.concatenate([high, low], 0))
    modes_x = dot(fwd_x[...], jnp.concatenate(cols, 1))
    modes_x = modes_x[:64] + modes_x[64:]
    modes = []
    for q in range(8):
        part = modes_x[:, 128 * q : 128 * q + 128]
        part = part[:32] + sign * pltpu.roll(part[32:], 64, 1)
        mb[pl.ds(q, 32, stride=8), :] = part
        modes.append(part)

    def dp_copy(target):
        return pltpu.make_async_remote_copy(
            src_ref=mb.at[pl.ds(pl.multiple_of(target * 32, 32), 32)],
            dst_ref=wgr.at[pl.ds(pl.multiple_of(dp * 32, 32), 32)],
            send_sem=send_sem.at[1],
            recv_sem=recv_sem.at[1],
            device_id={"dp": target},
            device_id_type=MESH,
        )

    @pl.loop(1, DP)
    def _(step):
        dp_copy(lax.rem(dp + step, DP)).start()

    ours = pl.ds(pl.multiple_of(dp * 32, 32), 32)
    wgr[ours, :] = mb[ours, :]

    later[0].wait()
    high, low = split(jnp.concatenate(modes, 0))
    spread = dot(jnp.concatenate([high, low], 1), spread_cot[...])
    for q in range(8):
        cr = spread[32 * q : 32 * q + 32, :128]
        ci = spread[32 * q : 32 * q + 32, 128:]
        for a in range(4):
            for g in range(2):
                col = 256 * a + 128 * g
                wr = wv[q, :, col : col + 128].astype(F32)
                wi = wv[q, :, 1024 + col : 1024 + col + 128].astype(F32)
                for r, value in enumerate((cr * wr + ci * wi, ci * wr - cr * wi)):
                    high, low = split(value)
                    cols = slice(128 * g, 128 * g + 128)
                    prod[2 * q + r, 32 * a : 32 * a + 32, cols] = high
                    prod[2 * q + r, 128 + 32 * a : 160 + 32 * a, cols] = low
    plain, turned = [], []
    for q in range(8):
        re, im = [dot_nt(sums[...], prod[2 * q + r]) for r in range(2)]
        re = re[:, :128] + re[:, 128:]
        im = im[:, :128] + im[:, 128:]
        plain += [re, im]
        turned += [-im, re]
    grad = jnp.concatenate([jnp.concatenate(plain, 0), jnp.concatenate(turned, 0)], 1)
    high, low = split(grad)
    back = dot_nt(inv_x[...], high)
    back = back[:256] + back[256:] + dot_nt(inv_x[:256], low)
    for a in range(4):
        sb[pl.ds(a, 64, stride=4), :] = back[64 * a : 64 * a + 64]

    sb3 = sb.reshape(64, 4, 128)
    rb3 = rb.reshape(64, 4, 128)

    def back_copy(target):
        return pltpu.make_async_remote_copy(
            src_ref=sb3.at[target],
            dst_ref=rb3.at[me],
            send_sem=send_sem.at[2],
            recv_sem=recv_sem.at[2],
            device_id={"gx": target},
            device_id_type=MESH,
        )

    @pl.loop(0, GX - 1, unroll=9)
    def _(step):
        back_copy(far_first(me, step)).start()

    rb3[me] = sb3[me]

    dp_drain = pltpu.make_async_remote_copy(
        src_ref=mb.at[pl.ds(0, 224)], dst_ref=wgr.at[pl.ds(0, 224)],
        send_sem=send_sem.at[1], recv_sem=recv_sem.at[1],
        device_id={"dp": lax.rem(dp + 1, DP)}, device_id_type=MESH,
    )
    later[2].wait()
    dp_drain.wait_recv()
    high, low = split(wgr[...])
    pair = jnp.concatenate([high, low], 1)
    spread = dot(pair, spread_cot[...])
    cr = spread[:, :128]
    ci = spread[:, 128:]
    for j in range(8):
        inner = dot(pair, spread_in[j])
        ir = inner[:, :128]
        ii = inner[:, 128:]
        for r, value in enumerate((ir * cr + ii * ci, ir * ci - ii * cr)):
            total = value[0:32]
            for s in range(1, 8):
                total = total + value[32 * s : 32 * s + 32]
            at = 1024 * r + 128 * j
            wgs[at // 4 : at // 4 + 32, :] = total
    for q in range(8):
        for n in range(16):
            wg_ref[q, :, 128 * n : 128 * n + 128] = wgs[pl.ds(32 * n + q, 4, stride=8), :]

    inv_y_ref[...] = small[192:320, 0:192]
    later[1].wait()
    third = drain((sb, rb), pl.ds(0, 252), 2)
    third.wait_recv()
    back_ref[...] = rb[...]

    first.wait_send()
    dp_drain.wait_send()
    third.wait_send()


def finish_kernel(back_ref, lin, wg_ref, inv_z, inv_y, out_h, wg_h, out, sem):
    weights = pltpu.make_async_copy(wg_ref, wg_h, sem.at[4])
    weights.start()
    imag = (lax.broadcasted_iota(jnp.int32, (1, 128), 1) & 8) != 0
    tops, bottoms = [], []
    for n in range(8):
        value = back_ref[pl.ds(n, 32, stride=8), :]
        tops.append(value)
        bottoms.append(jnp.where(imag, pltpu.roll(value, 8, 1), -pltpu.roll(value, 120, 1)))
    stacked = jnp.concatenate([jnp.concatenate(tops, 1), jnp.concatenate(bottoms, 1)], 0)
    high, low = split(stacked)
    along = dot(inv_y[...], jnp.concatenate([high, low, high], 0))
    stores = []
    for a in range(4):
        value = jnp.concatenate(
            [along[:, 128 * a : 128 * a + 128], along[:, 512 + 128 * a : 640 + 128 * a]], 1
        )
        high, low = split(value)
        both = jnp.concatenate([high, low], 0)
        for n in range(4):
            part = dot(both, inv_z[:256, 256 * n : 256 * n + 256])
            total = part[:128] + part[128:] + dot(high, inv_z[256:, 256 * n : 256 * n + 256])
            for u in range(2):
                c = 8 * a + 2 * n + u
                out[c] = (total[:, 128 * u : 128 * u + 128] + lin[c]).astype(BF)
        rows = pl.ds(8 * a, 8)
        stores.append(pltpu.make_async_copy(out.at[rows], out_h.at[0, 0, rows], sem.at[a]))
        stores[-1].start()
    for copy in stores + [weights]:
        copy.wait()


def on_device(field, cotangent, spectral_weight, pointwise_weight):
    consts = [jnp.asarray(table) for table in tables()]
    operands = [field, cotangent, spectral_weight, pointwise_weight, *consts]
    hbm = pl.BlockSpec(memory_space=pltpu.HBM)
    vmem = pl.BlockSpec(memory_space=pltpu.VMEM)
    middle = pl.pallas_call(
        kernel,
        out_shape=(
            jax.ShapeDtypeStruct((256, 128), F32),
            jax.ShapeDtypeStruct((C, NY, NZ), F32),
            jax.ShapeDtypeStruct((8, 4, 2 * C * C), F32),
            jax.ShapeDtypeStruct((512, 1024), BF),
            jax.ShapeDtypeStruct((128, 192), BF),
        ),
        in_specs=[hbm] * 7,
        out_specs=(vmem,) * 5,
        scratch_shapes=[
            pltpu.VMEM((C, NY, NZ), BF),
            pltpu.VMEM((C, NY, NZ), BF),
            pltpu.VMEM((8, KX, 2 * C * C), BF),
            pltpu.VMEM((C, C), BF),
            pltpu.VMEM((1096, 256), BF),
            pltpu.VMEM((8, 256, 256), BF),
            pltpu.VMEM((4096, 128), F32),
            pltpu.VMEM((512, 128), F32),
            pltpu.VMEM((512, 128), F32),
            pltpu.VMEM((256, 128), F32),
            pltpu.VMEM((256, 128), F32),
            pltpu.VMEM((16, 256, 256), BF),
            pltpu.VMEM((256, 128), F32),
            pltpu.VMEM((256, 128), F32),
            pltpu.VMEM((512, 128), F32),
            pltpu.SemaphoreType.DMA((9,)),
            pltpu.SemaphoreType.DMA((3,)),
            pltpu.SemaphoreType.DMA((3,)),
        ],
        compiler_params=pltpu.CompilerParams(
            collective_id=0, has_side_effects=True, vmem_limit_bytes=40 << 20
        ),
        cost_estimate=pl.CostEstimate(flops=10**10, bytes_accessed=10**7, transcendentals=0),
    )(*[pltpu.with_memory_space_constraint(x, pltpu.HBM) for x in operands])
    return pl.pallas_call(
        finish_kernel,
        out_shape=(
            jax.ShapeDtypeStruct((1, 1, C, NY, NZ), BF),
            jax.ShapeDtypeStruct((8, 4, 2 * C * C), F32),
        ),
        in_specs=[vmem] * 5,
        out_specs=(hbm, hbm),
        scratch_shapes=[pltpu.VMEM((C, NY, NZ), BF), pltpu.SemaphoreType.DMA((5,))],
        compiler_params=pltpu.CompilerParams(vmem_limit_bytes=12 << 20),
        cost_estimate=pl.CostEstimate(flops=10**9, bytes_accessed=10**6, transcendentals=0),
    )(*middle)


def solution(mesh):
    placed = (
        P("dp", "gx", None, None, None),
        P("dp", "gx", None, None, None),
        P("gx", None, None),
        P(),
    )
    return jax.shard_map(
        on_device,
        mesh=mesh,
        in_specs=placed,
        out_specs=(P("dp", "gx", None, None, None), P("gx", "dp", None)),
        check_vma=False,
    )
```
